256 devices in a mesh: node: 64 (over z, x, core), sector: 4 (over y).
Axes of the slice: x: 4, y: 4, z: 8, core: 2. Of those that a mesh axis runs over, the one named last changes fastest.
Arguments:
- returns: bfloat16 [8192, 12, 2048], P('node'), may hold values from -0.29882812 to 0.29882812
- barrier_scale: float32 [8192, 12], P('node'), may hold values from 0.25 to 4
- parent_ids: int32 [8192, 1], P('node'), may hold values from 0 to 63; in each aligned block of 128 rows (0 to 127, 128 to 255, ...) at most 4 rows name the same one
- loadings: float32 [64, 2048], P('node'), may hold values from -3 to 3
- own_variance: float32 [64, 2048], P('node'), may hold values from 0.5 to 4
- sector_sizes: int32 [64], replicated, may hold values from 1 to 64, 2048 in all
Outputs:
- cholesky_rows: float32 [64, 2048, 2048], P('node', 'sector')
The draws below stay inside these ranges and needn't reach their ends.
Inputs may be any that keep to these rules, and one draw needn't show every extreme that they name: `parent_ids`: of the 128 children held by one index of node (aligned blocks of rows), at most 4 share a parent; in every draw some block has exactly 4 children of one parent. `sector_sizes`: the sizes sum to 2048, and the largest is 64.
All inputs are finite; a program needn't handle non-finite values.
Results may differ from the reference program's by a relative error of at most 0.00045.
Values may be sent and summed in bfloat16 or wider, within the bound.
A program may use at most 192 MiB of HBM per device.

```python
import math
import jax
import jax.numpy as jnp
import numpy as np
from jax import lax

N = 2048
SECT = 64
SECMAX = 64
K = 12
CHILD_DEV = 128
CAP = 4
PARENTS = 64
CHILDREN = 8192
N_NODE = 64


def level_of(key, dims, shards, low, high):
    def one(axis_at, parts):
        draws = jax.random.uniform(jax.random.fold_in(jax.random.fold_in(key, 6), axis_at), (parts,), jnp.float32, low / len(shards), high / len(shards))
        return jnp.repeat(jnp.exp(draws), dims[axis_at] // parts).reshape((-1,) + (1,) * (len(dims) - axis_at - 1))

    factor_of = one(*shards[0])
    for cut in shards[1:]:
        factor_of = factor_of * one(*cut)
    return factor_of


def profile(count, total, bound, skew):
    weights = [(1 << 20) // math.isqrt(grade ** skew) + 1 for grade in range(2, count + 1)]
    rest, holding = total - bound - (count - 1), [1] * (count - 1)
    while rest > 0:
        candidates = [i for i in range(count - 1) if holding[i] < bound]
        pool, remaining = sum([weights[i] for i in candidates]), rest
        for i in candidates:
            more = min(bound - holding[i], max(1, remaining * weights[i] // pool), rest)
            holding[i] = holding[i] + more
            rest = rest - more
    return np.array([bound] + holding)


def uneven(own_key, count, total, bound, lean):
    if count == 2:
        one = jax.random.randint(own_key, (), max(1, total - bound), min(bound, total - 1) + 1)
        return jnp.stack([one, total - one])
    tallies = jnp.asarray(profile(count, total, bound, lean), jnp.int32)
    pairs = (count - 1) // 2
    donor, taker = tallies[1:1 + 2 * pairs:2], tallies[2:2 + 2 * pairs:2]
    slack = jnp.minimum(donor - 1, bound - taker)
    moved = jax.random.randint(jax.random.fold_in(own_key, 1), (pairs,), 0, 1 << 20) % (slack + 1)
    tallies = tallies.at[1:1 + 2 * pairs:2].set(donor - moved).at[2:2 + 2 * pairs:2].set(taker + moved)
    return tallies[jax.random.permutation(jax.random.fold_in(own_key, 2), count)]


def routed_block(own_key, own, number, rows, amount, top, bound, slope):
    ranking = jax.random.permutation(own_key, amount)
    crowded, usual = portions_of(amount, rows * top, bound, slope, True), portions_of(amount, rows * top, bound, slope, False)
    places = jnp.arange(amount)

    def named(tallies, offset_by):
        used = int((tallies > 0).sum())
        fixed = max(1, used // 4)
        passed = fixed + (places - fixed + offset_by * (used - fixed)) % max(1, amount - fixed)
        return jnp.zeros((amount,), jnp.int32).at[ranking[jnp.where(places < fixed, places, passed)]].set(jnp.asarray(tallies, jnp.int32))

    tallies = jnp.where(number % 4 == 0, named(crowded, number // 4), named(usual, number - number // 4 - 1))
    mixed = jax.random.permutation(jax.random.fold_in(own, 3), amount)
    source_of, sink = mixed[0:amount // 2 * 2:2], mixed[1:amount // 2 * 2:2]
    slack = jnp.minimum(tallies[source_of] - 1, bound - tallies[sink]) // 2
    slack = jnp.where((source_of == ranking[0]) | (sink == ranking[0]) | (tallies[sink] == 0), 0, jnp.maximum(slack, 0))
    passed = jax.random.randint(jax.random.fold_in(own, 4), (amount // 2,), 0, 1 << 20) % (slack + 1)
    tallies = tallies.at[source_of].add(-passed).at[sink].add(passed)
    members = jnp.searchsorted(jnp.cumsum(tallies), jnp.arange(rows * top), side="right").astype(jnp.int32)
    listing = members.reshape(top, rows).T
    listing = listing[jax.random.permutation(jax.random.fold_in(own, 1), rows)]
    offset_by = jax.random.randint(jax.random.fold_in(own, 2), (rows, 1), 0, top)
    return jnp.take_along_axis(listing, (jnp.arange(top)[None, :] + offset_by) % top, axis=1)


def portions_of(count, total, reach, lean, full):
    portions = [(1 << 20) // math.isqrt(standing ** lean) + 1 for standing in range(1, count + 1)]
    largest = reach if full else min(reach, max(-(-total // count), total * portions[0] // sum(portions)))
    least = 1 if total - largest >= count - 1 else 0
    given, rest = [largest] + [least] * (count - 1), total - largest - least * (count - 1)
    while rest > 0:
        movable = [i for i in range(1, count) if given[i] < largest] or [i for i in range(1, count) if given[i] < reach]
        whole, left = sum([portions[i] for i in movable]), rest
        for i in movable:
            more = min(reach - given[i], max(1, left * portions[i] // whole), rest)
            given[i] = given[i] + more
            rest = rest - more
    return np.array(given)


def scatter_about(stream_key, dims, scale, limit, pieces=(), kind=jnp.bfloat16):
    drawn = scale * jax.random.normal(stream_key, dims, jnp.float32)
    if pieces:
        drawn = drawn * level_of(stream_key, dims, pieces, -0.22, 0.18)
    return jnp.clip(drawn, -limit, limit).astype(kind)


def setup_inputs(seed: int = 0) -> dict:
    streams_of = jax.random.split(jax.random.key(seed), 7)
    returns = scatter_about(streams_of[0], (CHILDREN, K, N), 0.05, 0.29882812, ((0, 64),))
    barrier_scale = jnp.clip(jnp.exp(math.log(4.0) - 2.7725887 * jax.random.uniform(streams_of[1], (CHILDREN, K), jnp.float32) ** level_of(streams_of[1], (CHILDREN, K), ((0, 64),), -0.2, 0.2)), 0.25, 4.0)
    parent_ids_keys = jax.random.split(jax.random.fold_in(streams_of[2], 1), CHILDREN // CHILD_DEV)
    parent_ids_turns = jax.random.permutation(jax.random.fold_in(streams_of[2], 3), CHILDREN // CHILD_DEV)
    parent_ids = jax.vmap(lambda own, number: routed_block(jax.random.fold_in(streams_of[2], 2), own, number, CHILD_DEV, PARENTS, 1, CAP, 2))(parent_ids_keys, parent_ids_turns).reshape((CHILDREN, 1))
    loadings = scatter_about(streams_of[3], (PARENTS, N), 0.5, 3.0, ((0, 64),), jnp.float32)
    own_variance = jnp.clip(jnp.exp(math.log(4.0) - 2.0794415 * jax.random.uniform(streams_of[4], (PARENTS, N), jnp.float32) ** level_of(streams_of[4], (PARENTS, N), ((0, 64),), -0.2, 0.2)), 0.5, 4.0)
    sector_sizes = uneven(streams_of[5], SECT, N, SECMAX, 1).astype(jnp.int32)
    return dict(returns=returns, barrier_scale=barrier_scale, parent_ids=parent_ids, loadings=loadings, own_variance=own_variance, sector_sizes=sector_sizes)


def sector_labels(sector_sizes, count):
    sector_ends = jnp.cumsum(sector_sizes).astype(jnp.int32)
    asset_index = jnp.arange(count, dtype=jnp.int32)
    return lax.optimization_barrier(jnp.sum((asset_index[:, None] >= sector_ends[None, :]).astype(jnp.int32), axis=1))

def reference(returns, barrier_scale, parent_ids, loadings, own_variance, sector_sizes):
    scaled = (jnp.sqrt(barrier_scale)[:, :, None] * returns.astype(jnp.float32)).astype(jnp.bfloat16)
    targets = parent_ids[:, 0].astype(jnp.int32)
    by_parent = jnp.argsort(targets, stable=True).astype(jnp.int32)
    parent_index = jnp.arange(PARENTS, dtype=jnp.int32)
    counts = lax.optimization_barrier(jnp.sum((targets[None, :] == parent_index[:, None]).astype(jnp.int32), axis=1))
    starts = (jnp.cumsum(counts) - counts).astype(jnp.int32)
    sector_of = sector_labels(sector_sizes, N)
    same_sector = sector_of[:, None] == sector_of[None, :]
    slot_count = N_NODE * CAP

    def factor_parent(parent):
        slots = jnp.arange(slot_count, dtype=jnp.int32)
        chosen = jnp.clip(starts[parent] + slots, 0, CHILDREN - 1).astype(jnp.int32)
        filled = slots < counts[parent]
        picked = scaled[by_parent[chosen]].astype(jnp.float32)
        picked = jnp.where(filled[:, None, None], picked, jnp.zeros((), jnp.float32))
        gathered_rows = picked.reshape(slot_count * K, N)
        schur = jnp.dot(gathered_rows.T.astype(jnp.float32), gathered_rows.astype(jnp.float32), precision=lax.Precision.HIGHEST, preferred_element_type=jnp.float32)
        loading = loadings[parent]
        covariance = jnp.where(same_sector, loading[:, None] * loading[None, :], jnp.zeros((), jnp.float32))
        normal_matrix = schur + covariance + jnp.diag(own_variance[parent])
        return jnp.linalg.cholesky(normal_matrix)
    return lax.map(factor_parent, parent_index)
```

```python
import functools

import jax
import jax.numpy as jnp
from jax import lax
from jax.experimental import pallas as pl
from jax.experimental.pallas import tpu as pltpu
from jax.sharding import PartitionSpec as P

F32 = jnp.float32
BF = jnp.bfloat16

def sub(x,k): return jnp.broadcast_to(x[k:k+1,:],(8,128))
def lane(x,k): return jnp.broadcast_to(x[:,k:k+1],(8,128))

def chol128(load, u_ref, inv_ref):
    row=lax.broadcasted_iota(jnp.int32,(8,128),0); col=lax.broadcasted_iota(jnp.int32,(8,128),1)
    wa=[load(g) for g in range(16)]
    wi=[jnp.where(col==row+8*g,1.0,0.0).astype(F32) for g in range(16)]
    for g in range(16):
        p,pi=wa[g],wi[g]
        nxt=g<15
        if nxt: r,ri=wa[g+1],wi[g+1]
        c=[lane(p,8*g+m) for m in range(8)]
        if nxt: cr=[lane(r,8*g+m) for m in range(8)]
        dvec=jnp.ones((8,128),F32)
        for k in range(8):
            dk=sub(c[k],k)
            inv=1.0/dk
            mk=jnp.where(row>k,c[k]*inv,0.0)
            prow,pirow=sub(p,k),sub(pi,k)
            if nxt: mr=cr[k]*inv
            for m in range(k+1,8):
                dkm=sub(c[m],k)
                c[m]=c[m]-mk*dkm
                if nxt: cr[m]=cr[m]-mr*dkm
            p=p-mk*prow; pi=pi-mk*pirow
            if nxt:
                r=r-mr*prow; ri=ri-mr*pirow
            dvec=jnp.where(row==k,dk,dvec)
        rs=lax.rsqrt(dvec)
        q=jnp.where(col>=row+8*g,p*rs,0.0); qi=pi*rs
        u_ref[8*g:8*g+8,:]=q; inv_ref[8*g:8*g+8,:]=qi
        if nxt: wa[g+1],wi[g+1]=r,ri
        if g<14:
            t=q.T
            qr=[sub(q,k) for k in range(8)]; qir=[sub(qi,k) for k in range(8)]
            for G in range(g+2,16):
                tg=t[8*G:8*G+8,:]
                a,b=wa[G],wi[G]
                for k in range(8):
                    tk=jnp.broadcast_to(tg[:,k:k+1],(8,128))
                    a=a-tk*qr[k]; b=b-tk*qir[k]
                wa[G],wi[G]=a,b


NT=(((1,),(1,)),((),()))
NN=(((1,),(0,)),((),()))
def dot(a,b,dims): return lax.dot_general(a,b,dims,preferred_element_type=F32)
def split(x):
    h=x.astype(BF); return h,(x-h.astype(F32)).astype(BF)
def dot3(a,b,dims):
    ah,al=split(a); bh,bl=split(b)
    return dot(ah,bh,dims)+(dot(al,bh,dims)+dot(ah,bl,dims))

def kern(mode, n, rows, s_ref, r_ref, lrow, lcol, frow, fcol, vrow, o_ref, a, rt, xl, xr, u0, i0, u1, i1, inv):
    nt=n//256
    ir=lax.broadcasted_iota(jnp.int32,(256,256),0); ic=lax.broadcasted_iota(jnp.int32,(256,256),1)
    eye=jnp.where(ir==ic,1.0,0.0)
    eyeb=eye.astype(BF)
    def al(x,m): return pl.multiple_of(x,m)
    def strip(i): return r_ref.at[i//2, :, pl.ds(al((i%2)*256,256),256)]
    if "S" in mode:
        def srow(i,_):
            src=strip(i)
            for kk in range(rows//512):
                rt[:,kk*512:(kk+1)*512]=dot(eyeb,src[kk*512:(kk+1)*512,:],NT).astype(BF)
            ri=pl.ds(al(i*256,256),256)
            lc=jnp.broadcast_to(lcol[ri,0:1],(256,256)); fc=jnp.broadcast_to(fcol[ri,0:1],(256,256))
            def scol(k,_):
                ki=pl.ds(al(k*256,256),256)
                s=dot(rt[...],strip(k)[...],NN)
                s=s+jnp.where(lc==lrow[:,ki],fc*frow[:,ki],0.0)
                s=s+jnp.where((ir==ic)&(i==k),vrow[:,ki],0.0)
                a[ri,ki]=s
                return 0
            lax.fori_loop(0,i+1,scol,0)
            return 0
        lax.fori_loop(0,nt,srow,0)
    if "C" in mode:
        def panel(p,_):
            c0=al(p*256,256); c1=al(p*256+128,128)
            chol128(lambda g:a[pl.ds(al(c0+8*g,8),8),pl.ds(c0,128)], u0, i0)
            x10=dot3(a[pl.ds(c1,128),pl.ds(c0,128)],i0[...],NT)
            a[pl.ds(c1,128),pl.ds(c0,128)]=x10
            a[pl.ds(c1,128),pl.ds(c1,128)]=a[pl.ds(c1,128),pl.ds(c1,128)]-dot3(x10,x10,NT)
            a[pl.ds(c0,128),pl.ds(c0,128)]=u0[...].T
            chol128(lambda g:a[pl.ds(al(c1+8*g,8),8),pl.ds(c1,128)], u1, i1)
            a[pl.ds(c1,128),pl.ds(c1,128)]=u1[...].T
            m=-dot3(i1[...],dot3(x10,i0[...],NN),NN)
            def put(rs,cs,v):
                h,l=split(v)
                inv[rs:rs+128,cs:cs+128]=h; inv[rs:rs+128,256+cs:256+cs+128]=h; inv[rs:rs+128,512+cs:512+cs+128]=l
            z=jnp.zeros((128,128),F32)
            put(0,0,i0[...]); put(0,128,z); put(128,0,m); put(128,128,i1[...])
            def trsm(t,_):
                ti=pl.ds(al(t*256,256),256)
                h,l=split(a[ti,pl.ds(c0,256)])
                x=dot(jnp.concatenate([h,l,h],axis=1),inv[...],NT)
                a[ti,pl.ds(c0,256)]=x
                h,l=split(x)
                xl[ti,0:256]=h; xl[ti,256:512]=l; xl[ti,512:768]=h
                xr[ti,0:256]=h; xr[ti,256:512]=h; xr[ti,512:768]=l
                return 0
            lax.fori_loop(p+1,nt,trsm,0)
            def trail(t,_):
                ti=pl.ds(al(t*256,256),256)
                def inner(k,_):
                    ki=pl.ds(al(k*256,256),256)
                    a[ti,ki]=a[ti,ki]-dot(xl[ti,:],xr[ki,:],NT)
                    return 0
                lax.fori_loop(p+1,t+1,inner,0)
                return 0
            lax.fori_loop(p+1,nt,trail,0)
            return 0
        lax.fori_loop(0,nt,panel,0)
    s=s_ref[0]
    def outp(b,_):
        r0=al(s*512+b*64,64)
        rr=lax.broadcasted_iota(jnp.int32,(64,n),0)+r0; cc=lax.broadcasted_iota(jnp.int32,(64,n),1)
        o_ref[pl.ds(al(b*64,64),64),:]=jnp.where(cc<=rr,a[pl.ds(r0,64),:],0.0)
        return 0
    lax.fori_loop(0,8,outp,0)

def factor(sidx, r, labels, loading, variance, mode="SC"):
    n=labels.shape[0]; rows=r.shape[1]
    V=pl.BlockSpec(memory_space=pltpu.VMEM)
    return pl.pallas_call(functools.partial(kern,mode,n,rows),
        out_shape=jax.ShapeDtypeStruct((512,n),F32),
        in_specs=[pl.BlockSpec(memory_space=pltpu.SMEM)]+[V]*6, out_specs=V,
        scratch_shapes=[pltpu.VMEM((n,n),F32),pltpu.VMEM((256,rows),BF),pltpu.VMEM((n,768),BF),pltpu.VMEM((n,768),BF)]
          +[pltpu.VMEM((128,128),F32)]*4+[pltpu.VMEM((256,768),BF)],
        compiler_params=pltpu.CompilerParams(vmem_limit_bytes=62*1024*1024),
    )(sidx, r, labels[None,:], labels[:,None], loading[None,:], loading[:,None], variance[None,:])


def gather_kernel(capacity, idx_ref, x_ref, o_ref):
    rows = x_ref.shape[1]

    def target(t, _):
        pieces = []
        for c in range(capacity):
            child = idx_ref[t * capacity + c]
            block = x_ref[jnp.maximum(child, 0)].astype(F32)
            pieces.append(jnp.where(child >= 0, block, 0.0))
        height = capacity * rows
        o_ref[pl.ds(pl.multiple_of(t * height, 16), height), :] = jnp.concatenate(pieces, axis=0).astype(BF)
        return 0

    lax.fori_loop(0, idx_ref.shape[0] // capacity, target, 0)


def gather_rows(idx, x, capacity):
    return pl.pallas_call(
        functools.partial(gather_kernel, capacity),
        out_shape=jax.ShapeDtypeStruct((idx.shape[0] * x.shape[1], x.shape[2]), BF),
        in_specs=[pl.BlockSpec(memory_space=pltpu.SMEM), pl.BlockSpec(memory_space=pltpu.VMEM)],
        out_specs=pl.BlockSpec(memory_space=pltpu.VMEM),
    )(idx, x)


def sector_labels(sector_sizes, count):
    sector_ends = jnp.cumsum(sector_sizes)
    asset_index = jnp.arange(count, dtype=jnp.int32)
    return jnp.sum((asset_index[:, None] >= sector_ends[None, :]).astype(jnp.int32), axis=1)


def on_device(returns, barrier_scale, parent_ids, loadings, own_variance, sector_sizes):
    node_count = lax.axis_size("node")
    sector_count = lax.axis_size("sector")
    my_index = lax.axis_index("sector")
    child_count, row_count, asset_count = returns.shape
    capacity = 4
    band = asset_count // sector_count
    mine = lax.dynamic_slice_in_dim(returns, my_index * band, band, 2)
    scaled = (jnp.sqrt(barrier_scale)[:, :, None] * mine.astype(F32)).astype(BF)
    targets = parent_ids[:, 0]
    child_index = jnp.arange(child_count, dtype=jnp.int32)
    earlier = (targets[:, None] == targets[None, :]) & (child_index[None, :] < child_index[:, None])
    position = jnp.sum(earlier.astype(jnp.int32), axis=1)
    slot_of = targets * capacity + position
    slots = jnp.arange(node_count * capacity, dtype=jnp.int32)
    idx = jnp.max(jnp.where(slot_of[None, :] == slots[:, None], child_index[None, :], -1), axis=1)
    outbox = gather_rows(idx, scaled, capacity)
    inbox = lax.all_to_all(outbox, "node", split_axis=0, concat_axis=0, tiled=True)
    quarters = lax.all_gather(inbox, "sector", axis=0, tiled=False)
    labels = sector_labels(sector_sizes, asset_count)
    out = factor(my_index[None].astype(jnp.int32), quarters, labels, loadings[0], own_variance[0])
    return out[None]


def solution(mesh):
    in_specs = (
        P("node", None, None),
        P("node", None),
        P("node", None),
        P("node", None),
        P("node", None),
        P(),
    )
    return jax.shard_map(
        on_device, mesh=mesh, in_specs=in_specs, out_specs=P("node", "sector", None), check_vma=False
    )
```

```python
import functools

import jax
import jax.numpy as jnp
from jax import lax
from jax.experimental import pallas as pl
from jax.experimental.pallas import tpu as pltpu
from jax.sharding import PartitionSpec as P

F32 = jnp.float32
BF = jnp.bfloat16

def sub(x,k): return jnp.broadcast_to(x[k:k+1,:],(8,128))
def lane(x,k): return jnp.broadcast_to(x[:,k:k+1],(8,128))

def chol128(load, u_ref, inv_ref):
    row=lax.broadcasted_iota(jnp.int32,(8,128),0); col=lax.broadcasted_iota(jnp.int32,(8,128),1)
    wa=[load(g) for g in range(16)]
    wi=[jnp.where(col==row+8*g,1.0,0.0).astype(F32) for g in range(16)]
    for g in range(16):
        p,pi=wa[g],wi[g]
        nxt=g<15
        if nxt: r,ri=wa[g+1],wi[g+1]
        c=[lane(p,8*g+m) for m in range(8)]
        if nxt: cr=[lane(r,8*g+m) for m in range(8)]
        dvec=jnp.ones((8,128),F32)
        for k in range(8):
            dk=sub(c[k],k)
            inv=1.0/dk
            mk=jnp.where(row>k,c[k]*inv,0.0)
            prow,pirow=sub(p,k),sub(pi,k)
            if nxt: mr=cr[k]*inv
            for m in range(k+1,8):
                dkm=sub(c[m],k)
                c[m]=c[m]-mk*dkm
                if nxt: cr[m]=cr[m]-mr*dkm
            p=p-mk*prow; pi=pi-mk*pirow
            if nxt:
                r=r-mr*prow; ri=ri-mr*pirow
            dvec=jnp.where(row==k,dk,dvec)
        rs=lax.rsqrt(dvec)
        q=jnp.where(col>=row+8*g,p*rs,0.0); qi=pi*rs
        u_ref[8*g:8*g+8,:]=q; inv_ref[8*g:8*g+8,:]=qi
        if nxt: wa[g+1],wi[g+1]=r,ri
        if g<14:
            t=q.T
            qr=[sub(q,k) for k in range(8)]; qir=[sub(qi,k) for k in range(8)]
            for G in range(g+2,16):
                tg=t[8*G:8*G+8,:]
                a,b=wa[G],wi[G]
                for k in range(8):
                    tk=jnp.broadcast_to(tg[:,k:k+1],(8,128))
                    a=a-tk*qr[k]; b=b-tk*qir[k]
                wa[G],wi[G]=a,b


NT=(((1,),(1,)),((),()))
NN=(((1,),(0,)),((),()))
def dot(a,b,dims): return lax.dot_general(a,b,dims,preferred_element_type=F32)
def split(x):
    h=x.astype(BF); return h,(x-h.astype(F32)).astype(BF)
def dot3(a,b,dims):
    ah,al=split(a); bh,bl=split(b)
    return dot(ah,bh,dims)+(dot(al,bh,dims)+dot(ah,bl,dims))

def kern(mode, n, rows, s_ref, r_ref, lrow, lcol, frow, fcol, vrow, o_ref, a, rt, xl, xr, u0, i0, u1, i1, inv):
    nt=n//256
    ir=lax.broadcasted_iota(jnp.int32,(256,256),0); ic=lax.broadcasted_iota(jnp.int32,(256,256),1)
    eye=jnp.where(ir==ic,1.0,0.0)
    eyeb=eye.astype(BF)
    def al(x,m): return pl.multiple_of(x,m)
    def strip(i): return r_ref.at[i]
    if "S" in mode:
        def srow(i,_):
            src=strip(i)
            for kk in range(rows//512):
                rt[:,kk*512:(kk+1)*512]=dot(eyeb,src[kk*512:(kk+1)*512,:],NT).astype(BF)
            ri=pl.ds(al(i*256,256),256)
            lc=jnp.broadcast_to(lcol[ri,0:1],(256,256)); fc=jnp.broadcast_to(fcol[ri,0:1],(256,256))
            def scol(k,_):
                ki=pl.ds(al(k*256,256),256)
                s=dot(rt[...],strip(k)[...],NN)
                s=s+jnp.where(lc==lrow[:,ki],fc*frow[:,ki],0.0)
                s=s+jnp.where((ir==ic)&(i==k),vrow[:,ki],0.0)
                a[ri,ki]=s
                return 0
            lax.fori_loop(0,i+1,scol,0)
            return 0
        lax.fori_loop(0,nt,srow,0)
    if "C" in mode:
        def panel(p,_):
            c0=al(p*256,256); c1=al(p*256+128,128)
            chol128(lambda g:a[pl.ds(al(c0+8*g,8),8),pl.ds(c0,128)], u0, i0)
            x10=dot3(a[pl.ds(c1,128),pl.ds(c0,128)],i0[...],NT)
            a[pl.ds(c1,128),pl.ds(c0,128)]=x10
            a[pl.ds(c1,128),pl.ds(c1,128)]=a[pl.ds(c1,128),pl.ds(c1,128)]-dot3(x10,x10,NT)
            a[pl.ds(c0,128),pl.ds(c0,128)]=u0[...].T
            chol128(lambda g:a[pl.ds(al(c1+8*g,8),8),pl.ds(c1,128)], u1, i1)
            a[pl.ds(c1,128),pl.ds(c1,128)]=u1[...].T
            m=-dot3(i1[...],dot3(x10,i0[...],NN),NN)
            def put(rs,cs,v):
                h,l=split(v)
                inv[rs:rs+128,cs:cs+128]=h; inv[rs:rs+128,256+cs:256+cs+128]=h; inv[rs:rs+128,512+cs:512+cs+128]=l
            z=jnp.zeros((128,128),F32)
            put(0,0,i0[...]); put(0,128,z); put(128,0,m); put(128,128,i1[...])
            def trsm(t,_):
                ti=pl.ds(al(t*256,256),256)
                h,l=split(a[ti,pl.ds(c0,256)])
                x=dot(jnp.concatenate([h,l,h],axis=1),inv[...],NT)
                a[ti,pl.ds(c0,256)]=x
                h,l=split(x)
                xl[ti,0:256]=h; xl[ti,256:512]=l; xl[ti,512:768]=h
                xr[ti,0:256]=h; xr[ti,256:512]=h; xr[ti,512:768]=l
                return 0
            lax.fori_loop(p+1,nt,trsm,0)
            def trail(t,_):
                ti=pl.ds(al(t*256,256),256)
                def inner(k,_):
                    ki=pl.ds(al(k*256,256),256)
                    a[ti,ki]=a[ti,ki]-dot(xl[ti,:],xr[ki,:],NT)
                    return 0
                lax.fori_loop(p+1,t+1,inner,0)
                return 0
            lax.fori_loop(p+1,nt,trail,0)
            return 0
        lax.fori_loop(0,nt,panel,0)
    s=s_ref[0]
    def outp(b,_):
        r0=al(s*512+b*64,64)
        rr=lax.broadcasted_iota(jnp.int32,(64,n),0)+r0; cc=lax.broadcasted_iota(jnp.int32,(64,n),1)
        o_ref[pl.ds(al(b*64,64),64),:]=jnp.where(cc<=rr,a[pl.ds(r0,64),:],0.0)
        return 0
    lax.fori_loop(0,8,outp,0)

def factor(sidx, r, labels, loading, variance, mode="SC"):
    n=labels.shape[0]; rows=r.shape[1]
    V=pl.BlockSpec(memory_space=pltpu.VMEM)
    return pl.pallas_call(functools.partial(kern,mode,n,rows),
        out_shape=jax.ShapeDtypeStruct((512,n),F32),
        in_specs=[pl.BlockSpec(memory_space=pltpu.SMEM)]+[V]*6, out_specs=V,
        scratch_shapes=[pltpu.VMEM((n,n),F32),pltpu.VMEM((256,rows),BF),pltpu.VMEM((n,768),BF),pltpu.VMEM((n,768),BF)]
          +[pltpu.VMEM((128,128),F32)]*4+[pltpu.VMEM((256,768),BF)],
        compiler_params=pltpu.CompilerParams(vmem_limit_bytes=62*1024*1024),
    )(sidx, r, labels[None,:], labels[:,None], loading[None,:], loading[:,None], variance[None,:])


MESH = pl.DeviceIdType.MESH
ORDER = (0, 1, 7, 2, 6, 3, 5, 4)


def prep_kernel(s_ref, targets_ref, scale_ref, x_ref, o_ref):
    rows, children, width = x_ref.shape
    targets = targets_ref[...]
    across = jnp.broadcast_to(targets.astype(F32), (children, children))
    first = lax.broadcasted_iota(jnp.int32, (children, children), 0)
    second = lax.broadcasted_iota(jnp.int32, (children, children), 1)
    earlier = (across.T == across) & (first < second)
    position = jnp.sum(jnp.where(earlier, 1.0, 0.0), axis=0, keepdims=True).astype(jnp.int32)
    slot = targets * 4 + position
    scale = jnp.concatenate([scale_ref[...], jnp.zeros((16 - rows, children), F32)], axis=0).T
    count = o_ref.shape[1]
    out_row = lax.broadcasted_iota(jnp.int32, (count * 16, children), 0)
    row_slot = (out_row // 16) * 4 + out_row % 4
    hit = row_slot == jnp.broadcast_to(slot, (count * 16, children))
    lane_of = (out_row // 4) % 4
    picks = jnp.concatenate(
        [jnp.where(hit & (lane_of == k), 1.0, 0.0).astype(BF) for k in range(4)], axis=1
    )
    for quad in range(rows // 4):
        scaled = []
        for k in range(4):
            r = quad * 4 + k
            scaled.append((scale[:, r : r + 1] * x_ref[r].astype(F32)).astype(BF))
        moved = dot(picks, jnp.concatenate(scaled, axis=0), NN).astype(BF)
        for h in range(2):
            half = moved[:, h * 256 : (h + 1) * 256]
            o_ref[h, :, quad * 16 : (quad + 1) * 16, :] = half.reshape(count, 16, 256)


def prepare(sector, targets, scale, planes):
    rows, children, assets = planes.shape
    width = 512
    return pl.pallas_call(
        prep_kernel,
        out_shape=jax.ShapeDtypeStruct((2, 64, rows * 4, 256), BF),
        grid_spec=pltpu.PrefetchScalarGridSpec(
            num_scalar_prefetch=1,
            grid=(1,),
            in_specs=[
                pl.BlockSpec((1, children), lambda i, s: (0, 0)),
                pl.BlockSpec((rows, children), lambda i, s: (0, 0)),
                pl.BlockSpec((rows, children, width), lambda i, s: (0, 0, s[0])),
            ],
            out_specs=pl.BlockSpec((2, 64, rows * 4, 256), lambda i, s: (0, 0, 0, 0)),
        ),
    )(sector, targets, scale, planes)


def exchange_kernel(out_ref, r_ref, ls, ss, rs, ys, yr, zs, zr):
    n = lax.axis_index("node")
    s = lax.axis_index("sector")
    z, w = n // 8, n % 8
    up, down = (s + 1) % 4, (s + 3) % 4

    def plane(h, j, i):
        t = ((z + 8 - j) % 8) * 8 + (w + 8 - i) % 8
        return pltpu.make_async_remote_copy(
            out_ref.at[h, t], r_ref.at[2 * s + h, n], ss.at[h], rs.at[h, j],
            device_id=(t, s), device_id_type=MESH)

    def group(strip, j, there, send, recv):
        rows = pl.ds(((z + j) % 8) * 8, 8)
        return pltpu.make_async_remote_copy(
            r_ref.at[strip, rows], r_ref.at[strip, rows], send, recv,
            device_id=(n, there), device_id_type=MESH)

    def own(h, j, d):
        return group(2 * s + h, j, (up, down)[d], ys.at[d, h], yr.at[d, h, j])

    def arriving(h, j, d):
        return group(2 * ((down, up)[d]) + h, j, (up, down)[d], ys.at[d, h], yr.at[d, h, j])

    def relay(j, d):
        return group(2 * ((down, up)[d]) + d, j, (up, down)[d], zs.at[d], zr.at[d, j])

    def relayed(j, d):
        return group(2 * ((s + 2) % 4) + d, j, (up, down)[d], zs.at[d], zr.at[d, j])

    mine = [pltpu.make_async_copy(out_ref.at[h, n], r_ref.at[2 * s + h, n], ls.at[h]) for h in range(2)]
    for c in mine:
        c.start()
    for j in ORDER:
        def send(i, _, j=j):
            plane(0, j, i).start()
            plane(1, j, i).start()
            return 0
        lax.fori_loop(1 if j == 0 else 0, 8, send, 0)
    last = None
    for j in ORDER + (None,):
        if j is not None:
            for h in range(2):
                count = 7 if j == 0 else 8
                blocks = r_ref.at[2 * s + h, pl.ds(((z + j) % 8) * 8, count)]
                pltpu.make_async_remote_copy(
                    blocks, blocks, ss.at[h], rs.at[h, j], device_id=(n, up), device_id_type=MESH
                ).wait_recv()
                if j == 0:
                    mine[h].wait()
            for h in range(2):
                for d in range(2):
                    own(h, j, d).start()
        if last is not None:
            for d in range(2):
                arriving(d, last, d).wait_recv()
                relay(last, d).start()
        last = j
    for j in ORDER:
        for d in range(2):
            arriving(1 - d, j, d).wait_recv()
            relayed(j, d).wait_recv()
    for h in range(2):
        blocks = out_ref.at[h, pl.ds(0, 63)]
        pltpu.make_async_remote_copy(
            blocks, blocks, ss.at[h], rs.at[h, 0], device_id=(n, up), device_id_type=MESH
        ).wait_send()
    for d in range(2):
        for h in range(2):
            pltpu.make_async_remote_copy(
                r_ref.at[0], r_ref.at[0], ys.at[d, h], yr.at[d, h, 0], device_id=(n, up), device_id_type=MESH
            ).wait_send()
        pltpu.make_async_remote_copy(
            r_ref.at[0], r_ref.at[0], zs.at[d], zr.at[d, 0], device_id=(n, up), device_id_type=MESH
        ).wait_send()


def exchange(outbox):
    dma = pltpu.SemaphoreType.DMA
    return pl.pallas_call(
        exchange_kernel,
        out_shape=jax.ShapeDtypeStruct((8,) + outbox.shape[1:], BF),
        in_specs=[pl.BlockSpec(memory_space=pl.ANY)],
        out_specs=pl.BlockSpec(memory_space=pl.ANY),
        scratch_shapes=[dma((2,)), dma((2,)), dma((2, 8)), dma((2, 2)), dma((2, 2, 8)), dma((2,)), dma((2, 8))],
        compiler_params=pltpu.CompilerParams(has_side_effects=True),
    )(outbox)


def sector_labels(sector_sizes, count):
    sector_ends = jnp.cumsum(sector_sizes)
    asset_index = jnp.arange(count, dtype=jnp.int32)
    return jnp.sum((asset_index[:, None] >= sector_ends[None, :]).astype(jnp.int32), axis=1)


def on_device(returns, barrier_scale, parent_ids, loadings, own_variance, sector_sizes):
    child_count, row_count, asset_count = returns.shape
    sector = lax.axis_index("sector")[None].astype(jnp.int32)
    outbox = prepare(
        sector,
        parent_ids.reshape(1, child_count),
        jnp.sqrt(barrier_scale).T,
        returns.transpose(1, 0, 2),
    )
    strips = exchange(outbox)
    strips = strips.reshape(8, -1, 256)
    labels = sector_labels(sector_sizes, asset_count)
    out = factor(sector, strips, labels, loadings[0], own_variance[0])
    return out[None]


def solution(mesh):
    in_specs = (
        P("node", None, None),
        P("node", None),
        P("node", None),
        P("node", None),
        P("node", None),
        P(),
    )
    return jax.shard_map(
        on_device, mesh=mesh, in_specs=in_specs, out_specs=P("node", "sector", None), check_vma=False
    )
```

```python
import functools
import types

import jax
import jax.numpy as jnp
from jax import lax
from jax.experimental import pallas as pl
from jax.experimental.pallas import tpu as pltpu
from jax.sharding import PartitionSpec as P

F32 = jnp.float32
BF = jnp.bfloat16


def sub(x,k): return jnp.broadcast_to(x[k:k+1,:],(8,128))
def lane(x,k): return jnp.broadcast_to(x[:,k:k+1],(8,128))

def chol128(load, u_ref, inv_ref):
    row=lax.broadcasted_iota(jnp.int32,(8,128),0); col=lax.broadcasted_iota(jnp.int32,(8,128),1)
    wa=[load(g) for g in range(16)]
    wi=[jnp.where(col==row+8*g,1.0,0.0).astype(F32) for g in range(16)]
    for g in range(16):
        p,pi=wa[g],wi[g]
        nxt=g<15
        if nxt: r,ri=wa[g+1],wi[g+1]
        c=[lane(p,8*g+m) for m in range(8)]
        if nxt: cr=[lane(r,8*g+m) for m in range(8)]
        dvec=jnp.ones((8,128),F32)
        for k in range(8):
            dk=sub(c[k],k)
            inv=1.0/dk
            mk=jnp.where(row>k,c[k]*inv,0.0)
            prow,pirow=sub(p,k),sub(pi,k)
            if nxt: mr=cr[k]*inv
            for m in range(k+1,8):
                dkm=sub(c[m],k)
                c[m]=c[m]-mk*dkm
                if nxt: cr[m]=cr[m]-mr*dkm
            p=p-mk*prow; pi=pi-mk*pirow
            if nxt:
                r=r-mr*prow; ri=ri-mr*pirow
            dvec=jnp.where(row==k,dk,dvec)
        rs=lax.rsqrt(dvec)
        q=jnp.where(col>=row+8*g,p*rs,0.0); qi=pi*rs
        u_ref[8*g:8*g+8,:]=q; inv_ref[8*g:8*g+8,:]=qi
        if nxt: wa[g+1],wi[g+1]=r,ri
        if g<14:
            t=q.T
            qr=[sub(q,k) for k in range(8)]; qir=[sub(qi,k) for k in range(8)]
            for G in range(g+2,16):
                tg=t[8*G:8*G+8,:]
                a,b=wa[G],wi[G]
                for k in range(8):
                    tk=jnp.broadcast_to(tg[:,k:k+1],(8,128))
                    a=a-tk*qr[k]; b=b-tk*qir[k]
                wa[G],wi[G]=a,b


NT = (((1,), (1,)), ((), ()))
NN = (((1,), (0,)), ((), ()))


def dot(a, b, dims):
    return lax.dot_general(a, b, dims, preferred_element_type=F32)


def split(x):
    high = x.astype(BF)
    return high, (x - high.astype(F32)).astype(BF)


def dot3(a, b, dims):
    ah, al = split(a)
    bh, bl = split(b)
    return dot(ah, bh, dims) + (dot(al, bh, dims) + dot(ah, bl, dims))


def tile(i, size=256):
    return pl.ds(pl.multiple_of(i * size, size), size)


def span(start, size, m=128):
    return pl.ds(pl.multiple_of(start, m), size)


def make_normal(c, lo, hi):
    ir = lax.broadcasted_iota(jnp.int32, (256, 256), 0)
    ic = lax.broadcasted_iota(jnp.int32, (256, 256), 1)
    eye = jnp.where(ir == ic, 1.0, 0.0).astype(BF)
    depth = c.r.shape[1]

    def strip(i, _):
        for part in range(depth // 512):
            rows = slice(part * 512, (part + 1) * 512)
            c.rt[:, rows] = dot(eye, c.r[i, rows, :], NT).astype(BF)
        ri = tile(i)
        labels = jnp.broadcast_to(c.lcol[ri, 0:1], (256, 256))
        loading = jnp.broadcast_to(c.fcol[ri, 0:1], (256, 256))

        def block(k, _):
            ki = tile(k)
            total = dot(c.rt[...], c.r[k], NN)
            total = total + jnp.where(labels == c.lrow[:, ki], loading * c.frow[:, ki], 0.0)
            total = total + jnp.where((ir == ic) & (i == k), c.vrow[:, ki], 0.0)
            c.a[ri, ki] = total
            return 0

        lax.fori_loop(0, i + 1, block, 0)
        return 0

    lax.fori_loop(lo, hi, strip, 0)


def diagonal(c, p, event):
    c0, c1 = span(p * 256, 128), span(p * 256 + 128, 128)
    event(2 * p)
    chol128(lambda g: c.a[span(p * 256 + 8 * g, 8, 8), c0], c.u, c.i0)
    c.a[c0, c0] = c.u[...].T
    below = dot3(c.a[c1, c0], c.i0[...], NT)
    c.a[c1, c0] = below
    c.a[c1, c1] = c.a[c1, c1] - dot3(below, below, NT)
    event(2 * p + 1)
    chol128(lambda g: c.a[span(p * 256 + 128 + 8 * g, 8, 8), c1], c.u, c.i1)
    c.a[c1, c1] = c.u[...].T
    corner = -dot3(c.i1[...], dot3(below, c.i0[...], NN), NN)
    zero = jnp.zeros((128, 128), F32)
    for rs, cs, v in ((0, 0, c.i0[...]), (0, 128, zero), (128, 0, corner), (128, 128, c.i1[...])):
        high, low = split(v)
        for at, part in ((0, high), (256, high), (512, low)):
            c.inv[p, rs : rs + 128, at + cs : at + cs + 128] = part


def solve(c, p, lo, hi):
    def one(t, _):
        ti, pi = tile(t), tile(p)
        high, low = split(c.a[ti, pi])
        x = dot(jnp.concatenate([high, low, high], axis=1), c.inv[p], NT)
        c.a[ti, pi] = x
        high, low = split(x)
        c.lh[ti, pi] = high
        c.ll[ti, pi] = low
        return 0

    lax.fori_loop(lo, hi, one, 0)


def update(c, p, lo, hi):
    def one(t, _):
        ti, pi = tile(t), tile(p)

        def block(k, _):
            ki = tile(k)
            high, low = c.lh[ti, pi], c.ll[ti, pi]
            other, other_low = c.lh[ki, pi], c.ll[ki, pi]
            c.a[ti, ki] = c.a[ti, ki] - dot(
                jnp.concatenate([high, low, high], axis=1),
                jnp.concatenate([other, other, other_low], axis=1), NT)
            return 0

        lax.fori_loop(p + 1, t + 1, block, 0)
        return 0

    lax.fori_loop(lo, hi, one, 0)


def write_band(c, s):
    n = c.a.shape[1]

    def rows(b, _):
        r0 = s * 512 + b * 64
        rr = lax.broadcasted_iota(jnp.int32, (64, n), 0) + r0
        cc = lax.broadcasted_iota(jnp.int32, (64, n), 1)
        c.o[tile(b, 64), :] = jnp.where(cc <= rr, c.a[span(r0, 64, 64), :], 0.0)
        return 0

    lax.fori_loop(0, 8, rows, 0)


def factor_scratch(n, rows):
    return dict(
        a=pltpu.VMEM((n, n), F32), rt=pltpu.VMEM((256, rows), BF),
        lh=pltpu.VMEM((n, n), BF), ll=pltpu.VMEM((n, n), BF),
        u=pltpu.VMEM((128, 128), F32), i0=pltpu.VMEM((128, 128), F32), i1=pltpu.VMEM((128, 128), F32),
        inv=pltpu.VMEM((n // 256, 256, 768), BF),
    )


def factor_steps(c, event, second):
    make_normal(c, 0, 4)

    def panel(p, _):
        hi = 4 + 4 * (p // 4)
        diagonal(c, p, event)
        solve(c, p, p + 1, hi)
        update(c, p, p + 1, hi)

        @pl.when(p == 3)
        def _():
            second()
            make_normal(c, 4, 8)

            def again(q, _):
                solve(c, q, 4, 8)
                update(c, q, 4, 8)
                return 0

            lax.fori_loop(0, 4, again, 0)

        return 0

    lax.fori_loop(0, 8, panel, 0)


MESH = pl.DeviceIdType.MESH


def prep_kernel(s_ref, targets_ref, scale_ref, x0_ref, x1_ref, o_ref):
    rows, children, width = x0_ref.shape
    targets = targets_ref[...]
    across = jnp.broadcast_to(targets.astype(F32), (children, children))
    first = lax.broadcasted_iota(jnp.int32, (children, children), 0)
    second = lax.broadcasted_iota(jnp.int32, (children, children), 1)
    earlier = (across.T == across) & (first < second)
    position = jnp.sum(jnp.where(earlier, 1.0, 0.0), axis=0, keepdims=True).astype(jnp.int32)
    slot = targets * 4 + position
    scale = jnp.concatenate([scale_ref[...], jnp.zeros((16 - rows, children), F32)], axis=0).T
    count = o_ref.shape[1]
    out_row = lax.broadcasted_iota(jnp.int32, (count * 16, children), 0)
    row_slot = (out_row // 16) * 4 + out_row % 4
    hit = row_slot == jnp.broadcast_to(slot, (count * 16, children))
    lane_of = (out_row // 4) % 4
    picks = jnp.concatenate(
        [jnp.where(hit & (lane_of == k), 1.0, 0.0).astype(BF) for k in range(4)], axis=1
    )
    for quad in range(rows // 4):
        for h, x_ref in enumerate((x0_ref, x1_ref)):
            scaled = []
            for k in range(4):
                r = quad * 4 + k
                scaled.append((scale[:, r : r + 1] * x_ref[r].astype(F32)).astype(BF))
            moved = dot(picks, jnp.concatenate(scaled, axis=0), NN).astype(BF)
            o_ref[h, :, quad * 16 : (quad + 1) * 16, :] = moved.reshape(count, 16, width)


def prepare(sector, targets, scale, planes):
    rows, children, assets = planes.shape
    width = 256
    return pl.pallas_call(
        prep_kernel,
        out_shape=jax.ShapeDtypeStruct((2, 64, rows * 4, 256), BF),
        grid_spec=pltpu.PrefetchScalarGridSpec(
            num_scalar_prefetch=1,
            grid=(1,),
            in_specs=[
                pl.BlockSpec((1, children), lambda i, s: (0, 0)),
                pl.BlockSpec((rows, children), lambda i, s: (0, 0)),
                pl.BlockSpec((rows, children, width), lambda i, s: (0, 0, s[0])),
                pl.BlockSpec((rows, children, width), lambda i, s: (0, 0, s[0] + 4)),
            ],
            out_specs=pl.BlockSpec((2, 64, rows * 4, 256), lambda i, s: (0, 0, 0, 0)),
        ),
    )(sector, targets, scale, planes, planes)


def sequence(q):
    return ((q % 2) * ((q + 1) // 2) + (1 - q % 2) * (8 - q // 2)) % 8


NAMES = ("a", "rt", "lh", "ll", "u", "i0", "i1", "inv")


def main_kernel(out_ref, lrow, lcol, frow, fcol, vrow, o_ref, r, ls, ss, rs, ys, yr, zs, zr, *scratch):
    n = lax.axis_index("node")
    s = lax.axis_index("sector")
    z, w = n // 8, n % 8
    up, down = (s + 1) % 4, (s + 3) % 4
    there = (up, down)
    c = types.SimpleNamespace(
        r=r, lrow=lrow, lcol=lcol, frow=frow, fcol=fcol, vrow=vrow, o=o_ref, **dict(zip(NAMES, scratch)))

    def send(h, q, i):
        t = ((z + 8 - sequence(q)) % 8) * 8 + (w + 8 - i) % 8
        pltpu.make_async_remote_copy(
            out_ref.at[h, t], r.at[4 * h + s, tile(n, 48)], ss.at[h], rs.at[h, q],
            device_id=(t, s), device_id_type=MESH).start()

    def landed(h, q, count):
        rows = r.at[4 * h + s, span(((z + sequence(q)) % 8) * 384, 48 * count, 48)]
        pltpu.make_async_remote_copy(
            rows, rows, ss.at[h], rs.at[h, q], device_id=(n, up), device_id_type=MESH).wait_recv()

    def group(strip, q, d, sent, got):
        rows = r.at[strip, tile((z + sequence(q)) % 8, 384)]
        return pltpu.make_async_remote_copy(
            rows, rows, sent, got, device_id=(n, there[d]), device_id_type=MESH)

    def own(h, q, d):
        return group(4 * h + s, q, d, ys.at[h, d], yr.at[h, d, q])

    def arriving(h, q, d):
        return group(4 * h + there[1 - d], q, d, ys.at[h, d], yr.at[h, d, q])

    def relay(h, q, d):
        return group(4 * h + there[1 - d], q, d, zs.at[h, d], zr.at[h, q])

    def relayed(h, q):
        return group(4 * h + (s + 2) % 4, q, 0, zs.at[h, 0], zr.at[h, q])

    def forward(h, q):
        for d in range(2):
            own(h, q, d).start()

    def pass_on(h, q, d):
        arriving(h, q, d).wait_recv()
        relay(h, q, d).start()

    def finish(h):
        def one(q, _):
            arriving(h, 2 * q, 1).wait_recv()
            arriving(h, 2 * q + 1, 0).wait_recv()
            relayed(h, 2 * q).wait_recv()
            relayed(h, 2 * q + 1).wait_recv()
            return 0

        lax.fori_loop(0, 4, one, 0)

    mine = [
        pltpu.make_async_copy(out_ref.at[h, n], r.at[4 * h + s, tile(n, 48)], ls.at[h]) for h in range(2)
    ]
    for m in mine:
        m.start()
    for h in range(2):
        def near(i, _, h=h):
            send(h, 0, i)
            return 0

        def far(q, _, h=h):
            def one(i, _):
                send(h, q, i)
                return 0

            lax.fori_loop(0, 8, one, 0)
            return 0

        lax.fori_loop(1, 8, near, 0)
        lax.fori_loop(1, 8, far, 0)

    landed(0, 0, 7)
    mine[0].wait()
    forward(0, 0)
    landed(0, 1, 8)
    forward(0, 1)

    def step(e, _):
        for b in range(2):
            landed(0, 2 * e + b, 8)
            forward(0, 2 * e + b)
            pass_on(0, 2 * e - 2 + b, b)
        return 0

    lax.fori_loop(1, 4, step, 0)
    pass_on(0, 6, 0)
    pass_on(0, 7, 1)
    finish(0)

    def event(e):
        @pl.when(e == 0)
        def _():
            landed(1, 0, 7)
            mine[1].wait()
            forward(1, 0)
            landed(1, 1, 8)
            forward(1, 1)

        @pl.when((e > 0) & (e < 4))
        def _():
            for b in range(2):
                landed(1, 2 * e + b, 8)
                forward(1, 2 * e + b)

        @pl.when((e > 0) & (e < 5))
        def _():
            for b in range(2):
                pass_on(1, 2 * e - 2 + b, b)

    factor_steps(c, event, lambda: finish(1))
    write_band(c, s)

    for h in range(2):
        blocks = out_ref.at[h, pl.ds(0, 63)]
        pltpu.make_async_remote_copy(
            blocks, blocks, ss.at[h], rs.at[h, 0], device_id=(n, up), device_id_type=MESH
        ).wait_send()
        for d in range(2):
            pltpu.make_async_remote_copy(
                r.at[0], r.at[0], ys.at[h, d], yr.at[h, d, 0], device_id=(n, up), device_id_type=MESH
            ).wait_send()
            half = r.at[0, pl.ds(0, 1536)]
            pltpu.make_async_remote_copy(
                half, half, zs.at[h, d], zr.at[h, 0], device_id=(n, up), device_id_type=MESH
            ).wait_send()


def exchange_and_factor(outbox, labels, loading, variance):
    dma = pltpu.SemaphoreType.DMA
    n = labels.shape[0]
    rows = outbox.shape[1] * outbox.shape[2]
    vmem = pl.BlockSpec(memory_space=pltpu.VMEM)
    scratch = factor_scratch(n, rows)
    return pl.pallas_call(
        main_kernel,
        out_shape=jax.ShapeDtypeStruct((n // 4, n), F32),
        in_specs=[pl.BlockSpec(memory_space=pl.ANY)] + [vmem] * 5,
        out_specs=vmem,
        scratch_shapes=[pltpu.VMEM((8, rows, 256), BF), dma((2,)), dma((2,)), dma((2, 8)), dma((2, 2)),
                        dma((2, 2, 8)), dma((2, 2)), dma((2, 8))] + [scratch[k] for k in NAMES],
        compiler_params=pltpu.CompilerParams(has_side_effects=True, vmem_limit_bytes=63 * 1024 * 1024),
    )(outbox, labels[None, :], labels[:, None], loading[None, :], loading[:, None], variance[None, :])


def sector_labels(sector_sizes, count):
    sector_ends = jnp.cumsum(sector_sizes)
    asset_index = jnp.arange(count, dtype=jnp.int32)
    return jnp.sum((asset_index[:, None] >= sector_ends[None, :]).astype(jnp.int32), axis=1)


def on_device(returns, barrier_scale, parent_ids, loadings, own_variance, sector_sizes):
    child_count, row_count, asset_count = returns.shape
    sector = lax.axis_index("sector")[None].astype(jnp.int32)
    outbox = prepare(
        sector,
        parent_ids.reshape(1, child_count),
        jnp.sqrt(barrier_scale).T,
        returns.transpose(1, 0, 2),
    )
    labels = sector_labels(sector_sizes, asset_count)
    out = exchange_and_factor(outbox, labels, loadings[0], own_variance[0])
    return out[None]


def solution(mesh):
    in_specs = (
        P("node", None, None),
        P("node", None),
        P("node", None),
        P("node", None),
        P("node", None),
        P(),
    )
    return jax.shard_map(
        on_device, mesh=mesh, in_specs=in_specs, out_specs=P("node", "sector", None), check_vma=False
    )
```

```python
import functools
import types

import jax
import jax.numpy as jnp
from jax import lax
from jax.experimental import pallas as pl
from jax.experimental.pallas import tpu as pltpu
from jax.sharding import PartitionSpec as P

F32 = jnp.float32
BF = jnp.bfloat16


def sub(x, k):
    return jnp.broadcast_to(x[k : k + 1, :], (8, 128))


def lane(x, k):
    return jnp.broadcast_to(x[:, k : k + 1], (8, 128))


def eliminate(p, pi, near, g, row):
    c = [lane(p, 8 * g + m) for m in range(8)]
    cs = [[lane(a, 8 * g + m) for m in range(8)] for a, _ in near]
    near = [list(x) for x in near]
    pivots = jnp.ones((8, 128), F32)
    for k in range(0, 8, 2):
        a, b, d = sub(c[k], k), sub(c[k + 1], k), sub(c[k + 1], k + 1)
        det = a * d - b * b
        ia = 1.0 / a
        id1 = a * (1.0 / det)
        ratio = b * ia
        m0 = jnp.where(row > k, c[k] * ia, 0.0)
        m1 = jnp.where(row > k + 1, (c[k + 1] - c[k] * ratio) * id1, 0.0)
        p0, pi0 = sub(p, k), sub(pi, k)
        p1, pi1 = sub(p, k + 1) - ratio * p0, sub(pi, k + 1) - ratio * pi0
        es = {}
        for m in range(k + 2, 8):
            e0 = sub(c[m], k)
            es[m] = (e0, sub(c[m], k + 1) - ratio * e0)
            c[m] = c[m] - m0 * es[m][0] - m1 * es[m][1]
        p = p - m0 * p0 - m1 * p1
        pi = pi - m0 * pi0 - m1 * pi1
        for x, cr in zip(near, cs):
            n0 = cr[k] * ia
            n1 = (cr[k + 1] - cr[k] * ratio) * id1
            for m in range(k + 2, 8):
                cr[m] = cr[m] - n0 * es[m][0] - n1 * es[m][1]
            x[0] = x[0] - n0 * p0 - n1 * p1
            x[1] = x[1] - n0 * pi0 - n1 * pi1
        pivots = jnp.where(row == k, a, jnp.where(row == k + 1, det * ia, pivots))
    scale = lax.rsqrt(pivots)
    return p * scale, pi * scale, near


def chol128(load, u_ref, inv_ref):
    row = lax.broadcasted_iota(jnp.int32, (8, 128), 0)
    col = lax.broadcasted_iota(jnp.int32, (8, 128), 1)
    n = 4
    wa = [load(g) for g in range(16)]
    wi = [jnp.where(col == row + 8 * g, 1.0, 0.0).astype(F32) for g in range(16)]
    for start in range(0, 16, n):
        qs, qis = [], []
        for g in range(start, start + n):
            near = [(wa[x], wi[x]) for x in range(g + 1, start + n)]
            q, qi, near = eliminate(wa[g], wi[g], near, g, row)
            for x, (a, b) in zip(range(g + 1, start + n), near):
                wa[x], wi[x] = a, b
            q = jnp.where(col >= row + 8 * g, q, 0.0)
            u_ref[8 * g : 8 * g + 8, :] = q
            inv_ref[8 * g : 8 * g + 8, :] = qi
            qs.append(q)
            qis.append(qi)
        if start + n < 16:
            q = jnp.concatenate(qs, axis=0)
            full = jnp.concatenate([q, jnp.concatenate(qis, axis=0)], axis=1)
            qh = full.astype(BF)
            ql = (full - qh.astype(F32)).astype(BF)
            left = jnp.concatenate([qh[:, :128], ql[:, :128], qh[:, :128]], axis=0)
            right = jnp.concatenate([qh, qh, ql], axis=0)
            moved = lax.dot_general(left, right, (((0,), (0,)), ((), ())), preferred_element_type=F32)
            for x in range(start + n, 16):
                wa[x] = wa[x] - moved[8 * x : 8 * x + 8, :128]
                wi[x] = wi[x] - moved[8 * x : 8 * x + 8, 128:]


NT = (((1,), (1,)), ((), ()))
NN = (((1,), (0,)), ((), ()))


def dot(a, b, dims):
    return lax.dot_general(a, b, dims, preferred_element_type=F32)


def split(x):
    high = x.astype(BF)
    return high, (x - high.astype(F32)).astype(BF)


def dot3(a, b, dims):
    ah, al = split(a)
    bh, bl = split(b)
    return dot(ah, bh, dims) + (dot(al, bh, dims) + dot(ah, bl, dims))


def tile(i, size=256):
    return pl.ds(pl.multiple_of(i * size, size), size)


def span(start, size, m=128):
    return pl.ds(pl.multiple_of(start, m), size)


def column(row_ref, cols):
    return jnp.broadcast_to(row_ref[:, cols], (256, 256)).T


def make_normal(c, lo, hi):
    ir = lax.broadcasted_iota(jnp.int32, (256, 256), 0)
    ic = lax.broadcasted_iota(jnp.int32, (256, 256), 1)
    eye = jnp.where(ir == ic, 1.0, 0.0).astype(BF)
    depth = c.r.shape[1]

    def strip(i, _):
        for part in range(depth // 512):
            rows = slice(part * 512, (part + 1) * 512)
            c.rt[:, rows] = dot(eye, c.r[i, rows, :], NT).astype(BF)
        ri = tile(i)
        labels = column(c.lrow, ri)
        loading = column(c.frow, ri)

        def block(k, _):
            ki = tile(k)
            total = dot(c.rt[...], c.r[k], NN)
            total = total + jnp.where(labels == c.lrow[:, ki], loading * c.frow[:, ki], 0.0)
            total = total + jnp.where((ir == ic) & (i == k), c.vrow[:, ki], 0.0)
            c.a[ri, ki] = total
            return 0

        lax.fori_loop(0, i + 1, block, 0)
        return 0

    lax.fori_loop(lo, hi, strip, 0)


def start_normal(c, hi):
    ir = lax.broadcasted_iota(jnp.int32, (256, 256), 0)
    ic = lax.broadcasted_iota(jnp.int32, (256, 256), 1)

    def strip(i, _):
        ri = tile(i)
        labels = column(c.lrow, ri)
        loading = column(c.frow, ri)

        def block(k, _):
            ki = tile(k)
            total = jnp.where(labels == c.lrow[:, ki], loading * c.frow[:, ki], 0.0)
            c.a[ri, ki] = total + jnp.where((ir == ic) & (i == k), c.vrow[:, ki], 0.0)
            return 0

        lax.fori_loop(0, i + 1, block, 0)
        return 0

    lax.fori_loop(0, hi, strip, 0)


def add_rows(c, start, hi):
    ir = lax.broadcasted_iota(jnp.int32, (256, 256), 0)
    ic = lax.broadcasted_iota(jnp.int32, (256, 256), 1)
    eye = jnp.where(ir == ic, 1.0, 0.0).astype(BF)
    rows = span(start, 384)

    def strip(i, _):
        turned = dot(eye, c.r[i, rows, :], NT).astype(BF)
        c.rt[:, 0:384] = turned
        ri = tile(i)

        def block(k, _):
            ki = tile(k)
            c.a[ri, ki] = c.a[ri, ki] + dot(c.rt[:, 0:384], c.r[k, rows, :], NN)
            return 0

        lax.fori_loop(0, i + 1, block, 0)
        return 0

    lax.fori_loop(0, hi, strip, 0)


def diagonal(c, p):
    c0, c1 = span(p * 256, 128), span(p * 256 + 128, 128)
    chol128(lambda g: c.a[span(p * 256 + 8 * g, 8, 8), c0], c.u0, c.i0)
    below = dot3(c.a[c1, c0], c.i0[...], NT)
    c.a[c1, c1] = c.a[c1, c1] - dot3(below, below, NT)
    chol128(lambda g: c.a[span(p * 256 + 128 + 8 * g, 8, 8), c1], c.u1, c.i1)
    c.a[c1, c0] = below
    c.a[c0, c0] = c.u0[...].T
    c.a[c1, c1] = c.u1[...].T
    corner = -dot3(c.i1[...], dot3(below, c.i0[...], NN), NN)
    zero = jnp.zeros((128, 128), F32)
    for rs, cs, v in ((0, 0, c.i0[...]), (0, 128, zero), (128, 0, corner), (128, 128, c.i1[...])):
        high, low = split(v)
        for at, part in ((0, high), (256, high), (512, low)):
            c.inv[p, rs : rs + 128, at + cs : at + cs + 128] = part


def solved(c, v, q, rows, cols):
    high, low = split(v)
    x = dot(jnp.concatenate([high, low, high], axis=1), c.inv[q], NT)
    c.a[rows, cols] = x
    high, low = split(x)
    c.lh[rows, cols] = high
    c.ll[rows, cols] = low


def lower_left(c):
    for q in range(4):
        cols = slice(256 * q, 256 * q + 256)
        done = slice(0, 256 * q)

        def half(i, _, q=q, cols=cols, done=done):
            rows = span(1024 + 512 * i, 512)
            v = c.a[rows, cols]
            if q:
                high, low = c.lh[rows, done], c.ll[rows, done]
                other, other_low = c.lh[cols, done], c.ll[cols, done]
                v = v - dot(
                    jnp.concatenate([high, low, high], axis=1),
                    jnp.concatenate([other, other, other_low], axis=1), NT)
            solved(c, v, q, rows, cols)
            return 0

        lax.fori_loop(0, 2, half, 0)

    def rest(t, _):
        ti = tile(t)

        def block(k, _):
            ki = tile(k)
            high, low = c.lh[ti, 0:1024], c.ll[ti, 0:1024]
            other, other_low = c.lh[ki, 0:1024], c.ll[ki, 0:1024]
            c.a[ti, ki] = c.a[ti, ki] - dot(
                jnp.concatenate([high, low, high], axis=1),
                jnp.concatenate([other, other, other_low], axis=1), NT)
            return 0

        lax.fori_loop(4, t + 1, block, 0)
        return 0

    lax.fori_loop(4, 8, rest, 0)


def solve(c, p, lo, hi):
    def one(t, _):
        ti, pi = tile(t), tile(p)
        high, low = split(c.a[ti, pi])
        x = dot(jnp.concatenate([high, low, high], axis=1), c.inv[p], NT)
        c.a[ti, pi] = x
        high, low = split(x)
        c.lh[ti, pi] = high
        c.ll[ti, pi] = low
        return 0

    lax.fori_loop(lo, hi, one, 0)


def update(c, p, lo, hi):
    def one(t, _):
        ti, pi = tile(t), tile(p)

        def block(k, _):
            ki = tile(k)
            high, low = c.lh[ti, pi], c.ll[ti, pi]
            other, other_low = c.lh[ki, pi], c.ll[ki, pi]
            c.a[ti, ki] = c.a[ti, ki] - dot(
                jnp.concatenate([high, low, high], axis=1),
                jnp.concatenate([other, other, other_low], axis=1), NT)
            return 0

        lax.fori_loop(p + 1, t + 1, block, 0)
        return 0

    lax.fori_loop(lo, hi, one, 0)


def write_band(c, s):
    n = c.a.shape[1]

    def rows(b, _):
        r0 = s * 512 + b * 64
        rr = lax.broadcasted_iota(jnp.int32, (64, n), 0) + r0
        cc = lax.broadcasted_iota(jnp.int32, (64, n), 1)
        c.o[tile(b, 64), :] = jnp.where(cc <= rr, c.a[span(r0, 64, 64), :], 0.0)
        return 0

    lax.fori_loop(0, 8, rows, 0)


def factor_scratch(n, rows):
    square = pltpu.VMEM((128, 128), F32)
    return dict(
        a=pltpu.VMEM((n, n), F32), rt=pltpu.VMEM((256, rows), BF),
        lh=pltpu.VMEM((n, n), BF), ll=pltpu.VMEM((n, n), BF),
        u0=square, u1=square, i0=square, i1=square,
        inv=pltpu.VMEM((n // 256, 256, 768), BF),
    )


def factor_steps(c, event, second):
    def panel(p, _):
        hi = 4 + 4 * (p // 4)
        event(2 * p)
        diagonal(c, p)
        event(2 * p + 1)
        solve(c, p, p + 1, hi)
        update(c, p, p + 1, hi)

        @pl.when(p == 3)
        def _():
            second()
            make_normal(c, 4, 8)
            lower_left(c)

        return 0

    lax.fori_loop(0, 8, panel, 0)


MESH = pl.DeviceIdType.MESH


def prep_kernel(s_ref, targets_ref, scale_ref, x0_ref, x1_ref, o_ref):
    rows, children, width = x0_ref.shape
    targets = targets_ref[...]
    across = jnp.broadcast_to(targets.astype(F32), (children, children))
    first = lax.broadcasted_iota(jnp.int32, (children, children), 0)
    second = lax.broadcasted_iota(jnp.int32, (children, children), 1)
    earlier = (across.T == across) & (first < second)
    position = jnp.sum(jnp.where(earlier, 1.0, 0.0), axis=0, keepdims=True).astype(jnp.int32)
    slot = targets * 4 + position
    scale = jnp.concatenate([scale_ref[...], jnp.zeros((16 - rows, children), F32)], axis=0).T
    count = o_ref.shape[1]
    out_row = lax.broadcasted_iota(jnp.int32, (count * 16, children), 0)
    row_slot = (out_row // 16) * 4 + out_row % 4
    hit = row_slot == jnp.broadcast_to(slot, (count * 16, children))
    lane_of = (out_row // 4) % 4
    picks = jnp.concatenate(
        [jnp.where(hit & (lane_of == k), 1.0, 0.0).astype(BF) for k in range(4)], axis=1
    )
    for quad in range(rows // 4):
        for h, x_ref in enumerate((x0_ref, x1_ref)):
            scaled = []
            for k in range(4):
                r = quad * 4 + k
                scaled.append((scale[:, r : r + 1] * x_ref[r].astype(F32)).astype(BF))
            moved = dot(picks, jnp.concatenate(scaled, axis=0), NN).astype(BF)
            o_ref[h, :, quad * 16 : (quad + 1) * 16, :] = moved.reshape(count, 16, width)


def prepare(sector, targets, scale, planes):
    rows, children, assets = planes.shape
    width = 256
    return pl.pallas_call(
        prep_kernel,
        out_shape=jax.ShapeDtypeStruct((2, 64, rows * 4, 256), BF),
        grid_spec=pltpu.PrefetchScalarGridSpec(
            num_scalar_prefetch=1,
            grid=(1,),
            in_specs=[
                pl.BlockSpec((1, children), lambda i, s: (0, 0)),
                pl.BlockSpec((rows, children), lambda i, s: (0, 0)),
                pl.BlockSpec((rows, children, width), lambda i, s: (0, 0, s[0])),
                pl.BlockSpec((rows, children, width), lambda i, s: (0, 0, s[0] + 4)),
            ],
            out_specs=pl.BlockSpec((2, 64, rows * 4, 256), lambda i, s: (0, 0, 0, 0)),
        ),
    )(sector, targets, scale, planes, planes)


def sequence(q):
    return ((q % 2) * ((q + 1) // 2) + (1 - q % 2) * (8 - q // 2)) % 8


NAMES = ("a", "rt", "lh", "ll", "u0", "u1", "i0", "i1", "inv")


def main_kernel(out_ref, lrow, frow, vrow, o_ref, r, ls, ss, rs, ys, yr, zs, zr, *scratch):
    n = lax.axis_index("node")
    s = lax.axis_index("sector")
    z, w = n // 8, n % 8
    up, down = (s + 1) % 4, (s + 3) % 4
    there = (up, down)
    c = types.SimpleNamespace(
        r=r, lrow=lrow, frow=frow, vrow=vrow, o=o_ref, **dict(zip(NAMES, scratch)))

    def send(h, q, i):
        t = ((z + 8 - sequence(q)) % 8) * 8 + (w + 8 - i) % 8
        pltpu.make_async_remote_copy(
            out_ref.at[h, t], r.at[4 * h + s, tile(n, 48)], ss.at[h], rs.at[h, q],
            device_id=(t, s), device_id_type=MESH).start()

    def landed(h, q, count):
        rows = r.at[4 * h + s, span(((z + sequence(q)) % 8) * 384, 48 * count, 48)]
        pltpu.make_async_remote_copy(
            rows, rows, ss.at[h], rs.at[h, q], device_id=(n, up), device_id_type=MESH).wait_recv()

    def group(strip, q, d, sent, got):
        rows = r.at[strip, tile((z + sequence(q)) % 8, 384)]
        return pltpu.make_async_remote_copy(
            rows, rows, sent, got, device_id=(n, there[d]), device_id_type=MESH)

    def own(h, q, d):
        return group(4 * h + s, q, d, ys.at[h, d], yr.at[h, d, q])

    def arriving(h, q, d):
        return group(4 * h + there[1 - d], q, d, ys.at[h, d], yr.at[h, d, q])

    def relay(h, q, d):
        return group(4 * h + there[1 - d], q, d, zs.at[h, d], zr.at[h, q])

    def relayed(h, q):
        return group(4 * h + (s + 2) % 4, q, 0, zs.at[h, 0], zr.at[h, q])

    def forward(h, q):
        for d in range(2):
            own(h, q, d).start()

    def pass_on(h, q, d):
        arriving(h, q, d).wait_recv()
        relay(h, q, d).start()

    def finish():
        def one(q, _):
            arriving(1, 2 * q, 1).wait_recv()
            arriving(1, 2 * q + 1, 0).wait_recv()
            relayed(1, 2 * q).wait_recv()
            relayed(1, 2 * q + 1).wait_recv()
            return 0

        lax.fori_loop(0, 4, one, 0)

    mine = [
        pltpu.make_async_copy(out_ref.at[h, n], r.at[4 * h + s, tile(n, 48)], ls.at[h]) for h in range(2)
    ]
    for m in mine:
        m.start()
    for h in range(2):
        def near(i, _, h=h):
            send(h, 0, i)
            return 0

        def far(q, _, h=h):
            def one(i, _):
                send(h, q, i)
                return 0

            lax.fori_loop(0, 8, one, 0)
            return 0

        lax.fori_loop(1, 8, near, 0)
        lax.fori_loop(1, 8, far, 0)

    start_normal(c, 4)

    def gather(h, q, d):
        arriving(h, q, 1 - d).wait_recv()
        relayed(h, q).wait_recv()

    def add(e):
        for b in range(2):
            q = 2 * e + b
            gather(0, q, b)
            add_rows(c, ((z + sequence(q)) % 8) * 384, 4)

    landed(0, 0, 7)
    mine[0].wait()
    forward(0, 0)
    landed(0, 1, 8)
    forward(0, 1)

    def step(e, _):
        for b in range(2):
            landed(0, 2 * e + b, 8)
            forward(0, 2 * e + b)
            pass_on(0, 2 * e - 2 + b, b)

        @pl.when(e > 1)
        def _():
            add(e - 2)

        return 0

    lax.fori_loop(1, 4, step, 0)
    pass_on(0, 6, 0)
    pass_on(0, 7, 1)

    def rest(e, _):
        add(e)
        return 0

    lax.fori_loop(2, 4, rest, 0)

    def event(e):
        @pl.when(e == 0)
        def _():
            landed(1, 0, 7)
            mine[1].wait()
            forward(1, 0)
            landed(1, 1, 8)
            forward(1, 1)

        @pl.when((e > 0) & (e < 4))
        def _():
            for b in range(2):
                landed(1, 2 * e + b, 8)
                forward(1, 2 * e + b)

        @pl.when((e > 0) & (e < 5))
        def _():
            for b in range(2):
                pass_on(1, 2 * e - 2 + b, b)

    factor_steps(c, event, finish)
    write_band(c, s)

    for h in range(2):
        blocks = out_ref.at[h, pl.ds(0, 63)]
        pltpu.make_async_remote_copy(
            blocks, blocks, ss.at[h], rs.at[h, 0], device_id=(n, up), device_id_type=MESH
        ).wait_send()
        for d in range(2):
            pltpu.make_async_remote_copy(
                r.at[0], r.at[0], ys.at[h, d], yr.at[h, d, 0], device_id=(n, up), device_id_type=MESH
            ).wait_send()
            half = r.at[0, pl.ds(0, 1536)]
            pltpu.make_async_remote_copy(
                half, half, zs.at[h, d], zr.at[h, 0], device_id=(n, up), device_id_type=MESH
            ).wait_send()


def exchange_and_factor(outbox, labels, loading, variance):
    dma = pltpu.SemaphoreType.DMA
    n = labels.shape[0]
    rows = outbox.shape[1] * outbox.shape[2]
    vmem = pl.BlockSpec(memory_space=pltpu.VMEM)
    scratch = factor_scratch(n, rows)
    return pl.pallas_call(
        main_kernel,
        out_shape=jax.ShapeDtypeStruct((n // 4, n), F32),
        in_specs=[pl.BlockSpec(memory_space=pl.ANY)] + [vmem] * 3,
        out_specs=vmem,
        scratch_shapes=[pltpu.VMEM((8, rows, 256), BF), dma((2,)), dma((2,)), dma((2, 8)), dma((2, 2)),
                        dma((2, 2, 8)), dma((2, 2)), dma((2, 8))] + [scratch[k] for k in NAMES],
        compiler_params=pltpu.CompilerParams(has_side_effects=True, vmem_limit_bytes=63 * 1024 * 1024),
    )(outbox, labels.astype(F32)[None, :], loading[None, :], variance[None, :])


def sector_labels(sector_sizes, count):
    sector_ends = jnp.cumsum(sector_sizes)
    asset_index = jnp.arange(count, dtype=jnp.int32)
    return jnp.sum((asset_index[:, None] >= sector_ends[None, :]).astype(jnp.int32), axis=1)


def on_device(returns, barrier_scale, parent_ids, loadings, own_variance, sector_sizes):
    child_count, row_count, asset_count = returns.shape
    sector = lax.axis_index("sector")[None].astype(jnp.int32)
    outbox = prepare(
        sector,
        parent_ids.reshape(1, child_count),
        jnp.sqrt(barrier_scale).T,
        returns.transpose(1, 0, 2),
    )
    labels = sector_labels(sector_sizes, asset_count)
    out = exchange_and_factor(outbox, labels, loadings[0], own_variance[0])
    return out[None]


def solution(mesh):
    in_specs = (
        P("node", None, None),
        P("node", None),
        P("node", None),
        P("node", None),
        P("node", None),
        P(),
    )
    return jax.shard_map(
        on_device, mesh=mesh, in_specs=in_specs, out_specs=P("node", "sector", None), check_vma=False
    )
```

```python
import functools
import types

import jax
import jax.numpy as jnp
from jax import lax
from jax.experimental import pallas as pl
from jax.experimental.pallas import tpu as pltpu
from jax.sharding import PartitionSpec as P

F32 = jnp.float32
BF = jnp.bfloat16


def sub(x, k):
    return jnp.broadcast_to(x[k : k + 1, :], (8, 128))


def lane(x, k):
    return jnp.broadcast_to(x[:, k : k + 1], (8, 128))


def eliminate(p, pi, near, g, row):
    c = [lane(p, 8 * g + m) for m in range(8)]
    cs = [[lane(a, 8 * g + m) for m in range(8)] for a, _ in near]
    near = [list(x) for x in near]
    pivots = jnp.ones((8, 128), F32)
    for k in range(0, 8, 2):
        a, b, d = sub(c[k], k), sub(c[k + 1], k), sub(c[k + 1], k + 1)
        det = a * d - b * b
        ia = 1.0 / a
        id1 = a * (1.0 / det)
        ratio = b * ia
        m0 = jnp.where(row > k, c[k] * ia, 0.0)
        m1 = jnp.where(row > k + 1, (c[k + 1] - c[k] * ratio) * id1, 0.0)
        p0, pi0 = sub(p, k), sub(pi, k)
        p1, pi1 = sub(p, k + 1) - ratio * p0, sub(pi, k + 1) - ratio * pi0
        es = {}
        for m in range(k + 2, 8):
            e0 = sub(c[m], k)
            es[m] = (e0, sub(c[m], k + 1) - ratio * e0)
            c[m] = c[m] - m0 * es[m][0] - m1 * es[m][1]
        p = p - m0 * p0 - m1 * p1
        pi = pi - m0 * pi0 - m1 * pi1
        for x, cr in zip(near, cs):
            n0 = cr[k] * ia
            n1 = (cr[k + 1] - cr[k] * ratio) * id1
            for m in range(k + 2, 8):
                cr[m] = cr[m] - n0 * es[m][0] - n1 * es[m][1]
            x[0] = x[0] - n0 * p0 - n1 * p1
            x[1] = x[1] - n0 * pi0 - n1 * pi1
        pivots = jnp.where(row == k, a, jnp.where(row == k + 1, det * ia, pivots))
    scale = lax.rsqrt(pivots)
    return p * scale, pi * scale, near


def chol128(load, u_ref, inv_ref):
    row = lax.broadcasted_iota(jnp.int32, (8, 128), 0)
    col = lax.broadcasted_iota(jnp.int32, (8, 128), 1)
    n = 4
    wa = [load(g) for g in range(16)]
    wi = [jnp.where(col == row + 8 * g, 1.0, 0.0).astype(F32) for g in range(16)]
    for start in range(0, 16, n):
        qs, qis = [], []
        for g in range(start, start + n):
            near = [(wa[x], wi[x]) for x in range(g + 1, start + n)]
            q, qi, near = eliminate(wa[g], wi[g], near, g, row)
            for x, (a, b) in zip(range(g + 1, start + n), near):
                wa[x], wi[x] = a, b
            q = jnp.where(col >= row + 8 * g, q, 0.0)
            u_ref[8 * g : 8 * g + 8, :] = q
            inv_ref[8 * g : 8 * g + 8, :] = qi
            qs.append(q)
            qis.append(qi)
        if start + n < 16:
            q = jnp.concatenate(qs, axis=0)
            full = jnp.concatenate([q, jnp.concatenate(qis, axis=0)], axis=1)
            qh = full.astype(BF)
            ql = (full - qh.astype(F32)).astype(BF)
            left = jnp.concatenate([qh[:, :128], ql[:, :128], qh[:, :128]], axis=0)
            right = jnp.concatenate([qh, qh, ql], axis=0)
            moved = lax.dot_general(left, right, (((0,), (0,)), ((), ())), preferred_element_type=F32)
            for x in range(start + n, 16):
                wa[x] = wa[x] - moved[8 * x : 8 * x + 8, :128]
                wi[x] = wi[x] - moved[8 * x : 8 * x + 8, 128:]


NT = (((1,), (1,)), ((), ()))
NN = (((1,), (0,)), ((), ()))


def dot(a, b, dims):
    return lax.dot_general(a, b, dims, preferred_element_type=F32)


def split(x):
    high = x.astype(BF)
    return high, (x - high.astype(F32)).astype(BF)


def dot3(a, b, dims):
    ah, al = split(a)
    bh, bl = split(b)
    return dot(ah, bh, dims) + (dot(al, bh, dims) + dot(ah, bl, dims))


def tile(i, size=256):
    return pl.ds(pl.multiple_of(i * size, size), size)


def span(start, size, m=128):
    return pl.ds(pl.multiple_of(start, m), size)


def column(row_ref, cols):
    return jnp.broadcast_to(row_ref[:, cols], (256, 256)).T


def make_normal(c, lo, hi):
    ir = lax.broadcasted_iota(jnp.int32, (256, 256), 0)
    ic = lax.broadcasted_iota(jnp.int32, (256, 256), 1)
    eye = jnp.where(ir == ic, 1.0, 0.0).astype(BF)
    depth = c.r.shape[1]

    def strip(i, _):
        for part in range(depth // 512):
            rows = slice(part * 512, (part + 1) * 512)
            c.rt[:, rows] = dot(eye, c.r[i, rows, :], NT).astype(BF)
        ri = tile(i)
        labels = column(c.lrow, ri)
        loading = column(c.frow, ri)

        def block(k, _):
            ki = tile(k)
            total = dot(c.rt[...], c.r[k], NN)
            total = total + jnp.where(labels == c.lrow[:, ki], loading * c.frow[:, ki], 0.0)
            total = total + jnp.where((ir == ic) & (i == k), c.vrow[:, ki], 0.0)
            c.a[ri, ki] = total
            return 0

        lax.fori_loop(0, i + 1, block, 0)
        return 0

    lax.fori_loop(lo, hi, strip, 0)


def diagonal(c, p):
    c0, c1 = span(p * 256, 128), span(p * 256 + 128, 128)
    chol128(lambda g: c.a[span(p * 256 + 8 * g, 8, 8), c0], c.u0, c.i0)
    below = dot3(c.a[c1, c0], c.i0[...], NT)
    c.a[c1, c1] = c.a[c1, c1] - dot3(below, below, NT)
    chol128(lambda g: c.a[span(p * 256 + 128 + 8 * g, 8, 8), c1], c.u1, c.i1)
    c.a[c1, c0] = below
    c.a[c0, c0] = c.u0[...].T
    c.a[c1, c1] = c.u1[...].T
    corner = -dot3(c.i1[...], dot3(below, c.i0[...], NN), NN)
    zero = jnp.zeros((128, 128), F32)
    for rs, cs, v in ((0, 0, c.i0[...]), (0, 128, zero), (128, 0, corner), (128, 128, c.i1[...])):
        high, low = split(v)
        for at, part in ((0, high), (256, high), (512, low)):
            c.inv[p, rs : rs + 128, at + cs : at + cs + 128] = part


def finish_row(c, t):
    ti = tile(t)

    def panel(q, _):
        qi = tile(q)
        high, low = split(c.a[ti, qi])
        x = dot(jnp.concatenate([high, low, high], axis=1), c.inv[q], NT)
        c.a[ti, qi] = x
        high, low = split(x)
        c.lh[ti, qi] = high
        c.ll[ti, qi] = low

        def block(k, _):
            ki = tile(k)
            left, left_low = c.lh[ti, qi], c.ll[ti, qi]
            other, other_low = c.lh[ki, qi], c.ll[ki, qi]
            c.a[ti, ki] = c.a[ti, ki] - dot(
                jnp.concatenate([left, left_low, left], axis=1),
                jnp.concatenate([other, other, other_low], axis=1), NT)
            return 0

        lax.fori_loop(q + 1, t + 1, block, 0)
        return 0

    lax.fori_loop(0, t, panel, 0)


def write_band(c, s):
    n = c.a.shape[1]

    def rows(b, _):
        r0 = s * 512 + b * 64
        rr = lax.broadcasted_iota(jnp.int32, (64, n), 0) + r0
        cc = lax.broadcasted_iota(jnp.int32, (64, n), 1)
        c.o[tile(b, 64), :] = jnp.where(cc <= rr, c.a[span(r0, 64, 64), :], 0.0)
        return 0

    lax.fori_loop(0, 8, rows, 0)


def factor_scratch(n, rows):
    square = pltpu.VMEM((128, 128), F32)
    return dict(
        a=pltpu.VMEM((n, n), F32), rt=pltpu.VMEM((256, rows), BF),
        lh=pltpu.VMEM((n, n), BF), ll=pltpu.VMEM((n, n), BF),
        u0=square, u1=square, i0=square, i1=square,
        inv=pltpu.VMEM((n // 256, 256, 768), BF),
    )


def factor_steps(c, arrived, forward, pass_on):
    def row(t, _):
        arrived(t)
        make_normal(c, t, t + 1)
        forward(t + 2)
        finish_row(c, t)
        pass_on(t + 1)
        diagonal(c, t)
        return 0

    lax.fori_loop(0, 8, row, 0)


MESH = pl.DeviceIdType.MESH


def prep_kernel(at_ref, targets_ref, scale_ref, x_ref, o_ref, picks, scale):
    strip = pl.program_id(0)
    rows, children, width = x_ref.shape

    @pl.when(strip == 0)
    def _():
        targets = targets_ref[...]
        across = jnp.broadcast_to(targets.astype(F32), (children, children))
        first = lax.broadcasted_iota(jnp.int32, (children, children), 0)
        second = lax.broadcasted_iota(jnp.int32, (children, children), 1)
        earlier = (across.T == across) & (first < second)
        position = jnp.sum(jnp.where(earlier, 1.0, 0.0), axis=0, keepdims=True).astype(jnp.int32)
        slot = targets * 4 + position
        scale[...] = jnp.concatenate([scale_ref[...], jnp.zeros((16 - rows, children), F32)], axis=0).T
        height = picks.shape[0]
        out_row = lax.broadcasted_iota(jnp.int32, (height, children), 0)
        row_slot = (out_row // 16) * 4 + out_row % 4
        hit = row_slot == jnp.broadcast_to(slot, (height, children))
        lane_of = (out_row // 4) % 4
        for k in range(4):
            picks[:, k * children : (k + 1) * children] = jnp.where(hit & (lane_of == k), 1.0, 0.0).astype(BF)

    for quad in range(rows // 4):
        scaled = []
        for k in range(4):
            r = quad * 4 + k
            scaled.append((scale[:, r : r + 1] * x_ref[r].astype(F32)).astype(BF))
        scaled = jnp.concatenate(scaled, axis=0)
        for b in range(2):
            plane = lax.rem(at_ref[1] + 8 - (lax.rem(at_ref[0] + strip, 4) + 4 * b), 8)
            moved = dot(picks[span(plane * 128, 128), :], scaled, NN).astype(BF)
            o_ref[8 * b : 8 * b + 8, quad * 16 : (quad + 1) * 16, :] = moved.reshape(8, 16, width)


def prepare(at, targets, scale, planes):
    rows, children, assets = planes.shape
    width = 256
    return pl.pallas_call(
        prep_kernel,
        out_shape=jax.ShapeDtypeStruct((128, rows * 4, width), BF),
        grid_spec=pltpu.PrefetchScalarGridSpec(
            num_scalar_prefetch=1,
            grid=(assets // width,),
            in_specs=[
                pl.BlockSpec((1, children), lambda i, s: (0, 0)),
                pl.BlockSpec((rows, children), lambda i, s: (0, 0)),
                pl.BlockSpec((rows, children, width), lambda i, s: (0, 0, i)),
            ],
            out_specs=pl.BlockSpec((16, rows * 4, width), lambda i, s: (i, 0, 0)),
            scratch_shapes=[pltpu.VMEM((1024, 4 * children), BF), pltpu.VMEM((children, 16), F32)],
        ),
    )(at, targets, scale, planes)


NAMES = ("a", "rt", "lh", "ll", "u0", "u1", "i0", "i1", "inv")


def main_kernel(out_ref, lrow, frow, vrow, o_ref, r, ls, ss, rs, ys, yr, zs, zr, *scratch):
    n = lax.axis_index("node")
    s = lax.axis_index("sector")
    z, w = n // 8, n % 8
    there = ((s + 1) % 4, (s + 3) % 4)
    c = types.SimpleNamespace(
        r=r, lrow=lrow, frow=frow, vrow=vrow, o=o_ref, **dict(zip(NAMES, scratch)))

    def distance(t, b, sector):
        return (sector + t) % 4 + 4 * b

    def send(h, t, b, i):
        j = distance(t, b, s)
        other = (w + i) % 8
        pltpu.make_async_remote_copy(
            out_ref.at[(2 * t + b) * 8 + other], r.at[t, tile(n, 48)], ss.at[h], rs.at[t, b],
            device_id=(((z + 8 - j) % 8) * 8 + other, s), device_id_type=MESH).start()

    def landed(t, b, count):
        rows = r.at[t, span(((z + distance(t, b, s)) % 8) * 384, 48 * count, 48)]
        pltpu.make_async_remote_copy(
            rows, rows, ss.at[0], rs.at[t, b], device_id=(n, there[0]), device_id_type=MESH).wait_recv()

    def group(t, b, sector, d, sent, got):
        rows = r.at[t, tile((z + distance(t, b, sector)) % 8, 384)]
        return pltpu.make_async_remote_copy(
            rows, rows, sent, got, device_id=(n, there[d]), device_id_type=MESH)

    def own(t, b, d):
        return group(t, b, s, d, ys.at[d], yr.at[t, d, b])

    def arriving(t, b, d):
        return group(t, b, there[1 - d], d, ys.at[d], yr.at[t, d, b])

    def relay(t, b):
        return group(t, b, there[1 - b], b, zs.at[b], zr.at[t, b])

    def relayed(t, b):
        return group(t, b, (s + 2) % 4, b, zs.at[b], zr.at[t, b])

    def kept(h):
        t = (4 - s) % 4 + 4 * h
        return pltpu.make_async_copy(out_ref.at[16 * t + w], r.at[t, tile(n, 48)], ls.at[h])

    def forward(t):
        @pl.when(t < 8)
        def _():
            @pl.when(distance(t, 0, s) == 0)
            def _():
                landed(t, 0, 7)
                kept(t // 4).wait()

            @pl.when(distance(t, 0, s) > 0)
            def _():
                landed(t, 0, 8)

            own(t, 0, 0).start()
            own(t, 0, 1).start()
            landed(t, 1, 8)
            own(t, 1, 0).start()
            own(t, 1, 1).start()

    def pass_on(t):
        @pl.when(t < 8)
        def _():
            for b in range(2):
                arriving(t, b, b).wait_recv()
                relay(t, b).start()

    def arrived(t):
        for b in range(2):
            arriving(t, b, 1 - b).wait_recv()
            relayed(t, b).wait_recv()

    for h in range(2):
        kept(h).start()

        def strip(t, _, h=h):
            for b in range(2):
                def one(i, _, b=b):
                    send(h, t, b, i)
                    return 0

                lax.fori_loop((8 - distance(t, b, s)) // 8, 8, one, 0)
            return 0

        lax.fori_loop(4 * h, 4 * h + 4, strip, 0)

    forward(jnp.int32(0))
    forward(jnp.int32(1))
    pass_on(jnp.int32(0))
    factor_steps(c, arrived, forward, pass_on)
    write_band(c, s)

    for h in range(2):
        blocks = out_ref.at[pl.ds(0, 63)]
        pltpu.make_async_remote_copy(
            blocks, blocks, ss.at[h], rs.at[0, 0], device_id=(n, there[0]), device_id_type=MESH
        ).wait_send()
    for d in range(2):
        pair = r.at[pl.ds(0, 2)]
        pltpu.make_async_remote_copy(
            pair, pair, ys.at[d], yr.at[0, d, 0], device_id=(n, there[0]), device_id_type=MESH
        ).wait_send()
        pltpu.make_async_remote_copy(
            r.at[0], r.at[0], zs.at[d], zr.at[0, 0], device_id=(n, there[0]), device_id_type=MESH
        ).wait_send()


def exchange_and_factor(outbox, labels, loading, variance):
    dma = pltpu.SemaphoreType.DMA
    n = labels.shape[0]
    rows = outbox.shape[1] * 64
    vmem = pl.BlockSpec(memory_space=pltpu.VMEM)
    scratch = factor_scratch(n, rows)
    return pl.pallas_call(
        main_kernel,
        out_shape=jax.ShapeDtypeStruct((n // 4, n), F32),
        in_specs=[pl.BlockSpec(memory_space=pl.ANY)] + [vmem] * 3,
        out_specs=vmem,
        scratch_shapes=[pltpu.VMEM((8, rows, 256), BF), dma((2,)), dma((2,)), dma((8, 2)), dma((2,)),
                        dma((8, 2, 2)), dma((2,)), dma((8, 2))] + [scratch[k] for k in NAMES],
        compiler_params=pltpu.CompilerParams(has_side_effects=True, vmem_limit_bytes=63 * 1024 * 1024),
    )(outbox, labels.astype(F32)[None, :], loading[None, :], variance[None, :])


def sector_labels(sector_sizes, count):
    sector_ends = jnp.cumsum(sector_sizes)
    asset_index = jnp.arange(count, dtype=jnp.int32)
    return jnp.sum((asset_index[:, None] >= sector_ends[None, :]).astype(jnp.int32), axis=1)


def on_device(returns, barrier_scale, parent_ids, loadings, own_variance, sector_sizes):
    child_count, row_count, asset_count = returns.shape
    at = jnp.stack([lax.axis_index("sector"), lax.axis_index("node") // 8]).astype(jnp.int32)
    outbox = prepare(
        at,
        parent_ids.reshape(1, child_count),
        jnp.sqrt(barrier_scale).T,
        returns.transpose(1, 0, 2),
    )
    labels = sector_labels(sector_sizes, asset_count)
    out = exchange_and_factor(outbox, labels, loadings[0], own_variance[0])
    return out[None]


def solution(mesh):
    in_specs = (
        P("node", None, None),
        P("node", None),
        P("node", None),
        P("node", None),
        P("node", None),
        P(),
    )
    return jax.shard_map(
        on_device, mesh=mesh, in_specs=in_specs, out_specs=P("node", "sector", None), check_vma=False
    )
```

```python
import functools
import types

import jax
import jax.numpy as jnp
from jax import lax
from jax.experimental import pallas as pl
from jax.experimental.pallas import tpu as pltpu
from jax.sharding import PartitionSpec as P

F32 = jnp.float32
BF = jnp.bfloat16


def sub(x, k):
    return jnp.broadcast_to(x[k : k + 1, :], (8, 128))


def lane(x, k):
    return jnp.broadcast_to(x[:, k : k + 1], (8, 128))


def eliminate(p, pi, near, g, row):
    c = [lane(p, 8 * g + m) for m in range(8)]
    cs = [[lane(a, 8 * g + m) for m in range(8)] for a, _ in near]
    near = [list(x) for x in near]
    pivots = jnp.ones((8, 128), F32)
    for k in range(0, 8, 2):
        a, b, d = sub(c[k], k), sub(c[k + 1], k), sub(c[k + 1], k + 1)
        det = a * d - b * b
        ia = 1.0 / a
        id1 = a * (1.0 / det)
        ratio = b * ia
        m0 = jnp.where(row > k, c[k] * ia, 0.0)
        m1 = jnp.where(row > k + 1, (c[k + 1] - c[k] * ratio) * id1, 0.0)
        p0, pi0 = sub(p, k), sub(pi, k)
        p1, pi1 = sub(p, k + 1) - ratio * p0, sub(pi, k + 1) - ratio * pi0
        es = {}
        for m in range(k + 2, 8):
            e0 = sub(c[m], k)
            es[m] = (e0, sub(c[m], k + 1) - ratio * e0)
            c[m] = c[m] - m0 * es[m][0] - m1 * es[m][1]
        p = p - m0 * p0 - m1 * p1
        pi = pi - m0 * pi0 - m1 * pi1
        for x, cr in zip(near, cs):
            n0 = cr[k] * ia
            n1 = (cr[k + 1] - cr[k] * ratio) * id1
            for m in range(k + 2, 8):
                cr[m] = cr[m] - n0 * es[m][0] - n1 * es[m][1]
            x[0] = x[0] - n0 * p0 - n1 * p1
            x[1] = x[1] - n0 * pi0 - n1 * pi1
        pivots = jnp.where(row == k, a, jnp.where(row == k + 1, det * ia, pivots))
    scale = lax.rsqrt(pivots)
    return p * scale, pi * scale, near


def chol128(load, u_ref, inv_ref):
    row = lax.broadcasted_iota(jnp.int32, (8, 128), 0)
    col = lax.broadcasted_iota(jnp.int32, (8, 128), 1)
    n = 4
    wa = [load(g) for g in range(16)]
    wi = [jnp.where(col == row + 8 * g, 1.0, 0.0).astype(F32) for g in range(16)]
    for start in range(0, 16, n):
        qs, qis = [], []
        for g in range(start, start + n):
            near = [(wa[x], wi[x]) for x in range(g + 1, start + n)]
            q, qi, near = eliminate(wa[g], wi[g], near, g, row)
            for x, (a, b) in zip(range(g + 1, start + n), near):
                wa[x], wi[x] = a, b
            q = jnp.where(col >= row + 8 * g, q, 0.0)
            u_ref[8 * g : 8 * g + 8, :] = q
            inv_ref[8 * g : 8 * g + 8, :] = qi
            qs.append(q)
            qis.append(qi)
        if start + n < 16:
            q = jnp.concatenate(qs, axis=0)
            full = jnp.concatenate([q, jnp.concatenate(qis, axis=0)], axis=1)
            qh = full.astype(BF)
            ql = (full - qh.astype(F32)).astype(BF)
            left = jnp.concatenate([qh[:, :128], ql[:, :128], qh[:, :128]], axis=0)
            right = jnp.concatenate([qh, qh, ql], axis=0)
            moved = lax.dot_general(left, right, (((0,), (0,)), ((), ())), preferred_element_type=F32)
            for x in range(start + n, 16):
                wa[x] = wa[x] - moved[8 * x : 8 * x + 8, :128]
                wi[x] = wi[x] - moved[8 * x : 8 * x + 8, 128:]


NT = (((1,), (1,)), ((), ()))
NN = (((1,), (0,)), ((), ()))


def dot(a, b, dims):
    return lax.dot_general(a, b, dims, preferred_element_type=F32)


def split(x):
    high = x.astype(BF)
    return high, (x - high.astype(F32)).astype(BF)


def dot3(a, b, dims):
    ah, al = split(a)
    bh, bl = split(b)
    return dot(ah, bh, dims) + (dot(al, bh, dims) + dot(ah, bl, dims))


def tile(i, size=256):
    return pl.ds(pl.multiple_of(i * size, size), size)


def span(start, size, m=128):
    return pl.ds(pl.multiple_of(start, m), size)


def column(row_ref, cols):
    return jnp.broadcast_to(row_ref[:, cols], (256, 256)).T


def make_normal(c, lo, hi):
    ir = lax.broadcasted_iota(jnp.int32, (256, 256), 0)
    ic = lax.broadcasted_iota(jnp.int32, (256, 256), 1)
    eye = jnp.where(ir == ic, 1.0, 0.0).astype(BF)
    depth = c.r.shape[1]

    def strip(i, _):
        for part in range(depth // 512):
            rows = slice(part * 512, (part + 1) * 512)
            c.rt[:, rows] = dot(eye, c.r[i, rows, :], NT).astype(BF)
        ri = tile(i)
        labels = column(c.lrow, ri)
        loading = column(c.frow, ri)

        def block(k, _):
            ki = tile(k)
            total = dot(c.rt[...], c.r[k], NN)
            total = total + jnp.where(labels == c.lrow[:, ki], loading * c.frow[:, ki], 0.0)
            total = total + jnp.where((ir == ic) & (i == k), c.vrow[:, ki], 0.0)
            c.a[ri, ki] = total
            return 0

        lax.fori_loop(0, i + 1, block, 0)
        return 0

    lax.fori_loop(lo, hi, strip, 0)


def diagonal(c, p, between):
    c0, c1 = span(p * 256, 128), span(p * 256 + 128, 128)
    chol128(lambda g: c.a[span(p * 256 + 8 * g, 8, 8), c0], c.u0, c.i0)
    between()
    below = dot3(c.a[c1, c0], c.i0[...], NT)
    c.a[c1, c1] = c.a[c1, c1] - dot3(below, below, NT)
    chol128(lambda g: c.a[span(p * 256 + 128 + 8 * g, 8, 8), c1], c.u1, c.i1)
    c.a[c1, c0] = below
    c.a[c0, c0] = c.u0[...].T
    c.a[c1, c1] = c.u1[...].T
    corner = -dot3(c.i1[...], dot3(below, c.i0[...], NN), NN)
    zero = jnp.zeros((128, 128), F32)
    for rs, cs, v in ((0, 0, c.i0[...]), (0, 128, zero), (128, 0, corner), (128, 128, c.i1[...])):
        high, low = split(v)
        for at, part in ((0, high), (256, high), (512, low)):
            c.inv[p, rs : rs + 128, at + cs : at + cs + 128] = part


def finish_row(c, t):
    ti = tile(t)

    def panel(q, _):
        qi = tile(q)
        high, low = split(c.a[ti, qi])
        x = dot(jnp.concatenate([high, low, high], axis=1), c.inv[q], NT)
        c.a[ti, qi] = x
        high, low = split(x)
        c.lh[ti, qi] = high
        c.ll[ti, qi] = low

        def take_off(k, wide):
            ki = span(k * 256, wide)
            left, left_low = c.lh[ti, qi], c.ll[ti, qi]
            other, other_low = c.lh[ki, qi], c.ll[ki, qi]
            c.a[ti, ki] = c.a[ti, ki] - dot(
                jnp.concatenate([left, left_low, left], axis=1),
                jnp.concatenate([other, other, other_low], axis=1), NT)

        count = t - q

        @pl.when(count % 2 == 1)
        def _():
            take_off(q + 1, 256)

        def pair(e, _):
            take_off(q + 1 + count % 2 + 2 * e, 512)
            return 0

        lax.fori_loop(0, count // 2, pair, 0)
        return 0

    lax.fori_loop(0, t, panel, 0)


def write_band(c, s):
    n = c.a.shape[1]

    def rows(b, _):
        r0 = s * 512 + b * 64
        rr = lax.broadcasted_iota(jnp.int32, (64, n), 0) + r0
        cc = lax.broadcasted_iota(jnp.int32, (64, n), 1)
        c.o[tile(b, 64), :] = jnp.where(cc <= rr, c.a[span(r0, 64, 64), :], 0.0)
        return 0

    lax.fori_loop(0, 8, rows, 0)


def factor_scratch(n, rows):
    square = pltpu.VMEM((128, 128), F32)
    return dict(
        a=pltpu.VMEM((n, n), F32), rt=pltpu.VMEM((256, rows), BF),
        lh=pltpu.VMEM((n, n), BF), ll=pltpu.VMEM((n, n), BF),
        u0=square, u1=square, i0=square, i1=square,
        inv=pltpu.VMEM((n // 256, 256, 768), BF),
    )


def factor_steps(c, arrived, forward, pass_on):
    def row(t, _):
        arrived(t)
        forward(t + 2, 0)
        make_normal(c, t, t + 1)
        pass_on(t + 1, 1)
        finish_row(c, t)
        forward(t + 2, 1)
        diagonal(c, t, lambda: pass_on(t + 2, 0))
        return 0

    lax.fori_loop(0, 8, row, 0)


MESH = pl.DeviceIdType.MESH


def prep_kernel(at_ref, targets_ref, scale_ref, x_ref, o_ref, picks, scale):
    strip = pl.program_id(0)
    rows, children, width = x_ref.shape

    @pl.when(strip == 0)
    def _():
        targets = targets_ref[...]
        across = jnp.broadcast_to(targets.astype(F32), (children, children))
        first = lax.broadcasted_iota(jnp.int32, (children, children), 0)
        second = lax.broadcasted_iota(jnp.int32, (children, children), 1)
        earlier = (across.T == across) & (first < second)
        position = jnp.sum(jnp.where(earlier, 1.0, 0.0), axis=0, keepdims=True).astype(jnp.int32)
        slot = targets * 4 + position
        scale[...] = jnp.concatenate([scale_ref[...], jnp.zeros((16 - rows, children), F32)], axis=0).T
        height = picks.shape[0]
        out_row = lax.broadcasted_iota(jnp.int32, (height, children), 0)
        row_slot = (out_row // 16) * 4 + out_row % 4
        hit = row_slot == jnp.broadcast_to(slot, (height, children))
        lane_of = (out_row // 4) % 4
        for k in range(4):
            picks[:, k * children : (k + 1) * children] = jnp.where(hit & (lane_of == k), 1.0, 0.0).astype(BF)

    for quad in range(rows // 4):
        scaled = []
        for k in range(4):
            r = quad * 4 + k
            scaled.append((scale[:, r : r + 1] * x_ref[r].astype(F32)).astype(BF))
        scaled = jnp.concatenate(scaled, axis=0)
        for b in range(2):
            plane = lax.rem(at_ref[1] + 8 - (lax.rem(at_ref[0] + strip, 4) + 4 * b), 8)
            moved = dot(picks[span(plane * 128, 128), :], scaled, NN).astype(BF)
            o_ref[8 * b : 8 * b + 8, quad * 16 : (quad + 1) * 16, :] = moved.reshape(8, 16, width)


def prepare(at, targets, scale, planes):
    rows, children, assets = planes.shape
    width = 256
    return pl.pallas_call(
        prep_kernel,
        out_shape=jax.ShapeDtypeStruct((128, rows * 4, width), BF),
        grid_spec=pltpu.PrefetchScalarGridSpec(
            num_scalar_prefetch=1,
            grid=(assets // width,),
            in_specs=[
                pl.BlockSpec((1, children), lambda i, s: (0, 0)),
                pl.BlockSpec((rows, children), lambda i, s: (0, 0)),
                pl.BlockSpec((rows, children, width), lambda i, s: (0, 0, i)),
            ],
            out_specs=pl.BlockSpec((16, rows * 4, width), lambda i, s: (i, 0, 0)),
            scratch_shapes=[pltpu.VMEM((1024, 4 * children), BF), pltpu.VMEM((children, 16), F32)],
        ),
    )(at, targets, scale, planes)


NAMES = ("a", "rt", "lh", "ll", "u0", "u1", "i0", "i1", "inv")


def main_kernel(out_ref, lrow, frow, vrow, o_ref, r, ls, ss, rs, ys, yr, zs, zr, *scratch):
    n = lax.axis_index("node")
    s = lax.axis_index("sector")
    z, w = n // 8, n % 8
    there = ((s + 1) % 4, (s + 3) % 4)
    c = types.SimpleNamespace(
        r=r, lrow=lrow, frow=frow, vrow=vrow, o=o_ref, **dict(zip(NAMES, scratch)))

    def distance(t, b, sector):
        return (sector + t) % 4 + 4 * b

    def send(h, t, b, i):
        j = distance(t, b, s)
        other = (w + i) % 8
        pltpu.make_async_remote_copy(
            out_ref.at[(2 * t + b) * 8 + other], r.at[t, tile(n, 48)], ss.at[h], rs.at[t, b],
            device_id=(((z + 8 - j) % 8) * 8 + other, s), device_id_type=MESH).start()

    def landed(t, b, count):
        rows = r.at[t, span(((z + distance(t, b, s)) % 8) * 384, 48 * count, 48)]
        pltpu.make_async_remote_copy(
            rows, rows, ss.at[0], rs.at[t, b], device_id=(n, there[0]), device_id_type=MESH).wait_recv()

    def group(t, b, sector, d, sent, got):
        rows = r.at[t, tile((z + distance(t, b, sector)) % 8, 384)]
        return pltpu.make_async_remote_copy(
            rows, rows, sent, got, device_id=(n, there[d]), device_id_type=MESH)

    def own(t, b, d):
        return group(t, b, s, d, ys.at[d], yr.at[t, d, b])

    def arriving(t, b, d):
        return group(t, b, there[1 - d], d, ys.at[d], yr.at[t, d, b])

    def relay(t, b):
        return group(t, b, there[1 - b], b, zs.at[b], zr.at[t, b])

    def relayed(t, b):
        return group(t, b, (s + 2) % 4, b, zs.at[b], zr.at[t, b])

    def kept(h):
        t = (4 - s) % 4 + 4 * h
        return pltpu.make_async_copy(out_ref.at[16 * t + w], r.at[t, tile(n, 48)], ls.at[h])

    def forward(t, b):
        @pl.when(t < 8)
        def _():
            if b:
                landed(t, 1, 8)
            else:
                @pl.when(distance(t, 0, s) == 0)
                def _():
                    landed(t, 0, 7)
                    kept(t // 4).wait()

                @pl.when(distance(t, 0, s) > 0)
                def _():
                    landed(t, 0, 8)

            own(t, b, 0).start()
            own(t, b, 1).start()

    def pass_on(t, b):
        @pl.when(t < 8)
        def _():
            arriving(t, b, b).wait_recv()
            relay(t, b).start()

    def arrived(t):
        for b in range(2):
            arriving(t, b, 1 - b).wait_recv()
            relayed(t, b).wait_recv()

    for h in range(2):
        kept(h).start()

        def strip(t, _, h=h):
            for b in range(2):
                def one(i, _, b=b):
                    send(h, t, b, i)
                    return 0

                lax.fori_loop((8 - distance(t, b, s)) // 8, 8, one, 0)
            return 0

        lax.fori_loop(4 * h, 4 * h + 4, strip, 0)

    first, second = jnp.int32(0), jnp.int32(1)
    forward(first, 0)
    forward(first, 1)
    pass_on(first, 0)
    forward(second, 0)
    pass_on(first, 1)
    forward(second, 1)
    pass_on(second, 0)
    factor_steps(c, arrived, forward, pass_on)
    write_band(c, s)

    for h in range(2):
        blocks = out_ref.at[pl.ds(0, 63)]
        pltpu.make_async_remote_copy(
            blocks, blocks, ss.at[h], rs.at[0, 0], device_id=(n, there[0]), device_id_type=MESH
        ).wait_send()
    for d in range(2):
        pair = r.at[pl.ds(0, 2)]
        pltpu.make_async_remote_copy(
            pair, pair, ys.at[d], yr.at[0, d, 0], device_id=(n, there[0]), device_id_type=MESH
        ).wait_send()
        pltpu.make_async_remote_copy(
            r.at[0], r.at[0], zs.at[d], zr.at[0, 0], device_id=(n, there[0]), device_id_type=MESH
        ).wait_send()


def exchange_and_factor(outbox, labels, loading, variance):
    dma = pltpu.SemaphoreType.DMA
    n = labels.shape[0]
    rows = outbox.shape[1] * 64
    vmem = pl.BlockSpec(memory_space=pltpu.VMEM)
    scratch = factor_scratch(n, rows)
    return pl.pallas_call(
        main_kernel,
        out_shape=jax.ShapeDtypeStruct((n // 4, n), F32),
        in_specs=[pl.BlockSpec(memory_space=pl.ANY)] + [vmem] * 3,
        out_specs=vmem,
        scratch_shapes=[pltpu.VMEM((8, rows, 256), BF), dma((2,)), dma((2,)), dma((8, 2)), dma((2,)),
                        dma((8, 2, 2)), dma((2,)), dma((8, 2))] + [scratch[k] for k in NAMES],
        compiler_params=pltpu.CompilerParams(has_side_effects=True, vmem_limit_bytes=63 * 1024 * 1024),
    )(outbox, labels.astype(F32)[None, :], loading[None, :], variance[None, :])


def sector_labels(sector_sizes, count):
    sector_ends = jnp.cumsum(sector_sizes)
    asset_index = jnp.arange(count, dtype=jnp.int32)
    return jnp.sum((asset_index[:, None] >= sector_ends[None, :]).astype(jnp.int32), axis=1)


def on_device(returns, barrier_scale, parent_ids, loadings, own_variance, sector_sizes):
    child_count, row_count, asset_count = returns.shape
    at = jnp.stack([lax.axis_index("sector"), lax.axis_index("node") // 8]).astype(jnp.int32)
    outbox = prepare(
        at,
        parent_ids.reshape(1, child_count),
        jnp.sqrt(barrier_scale).T,
        returns.transpose(1, 0, 2),
    )
    labels = sector_labels(sector_sizes, asset_count)
    out = exchange_and_factor(outbox, labels, loadings[0], own_variance[0])
    return out[None]


def solution(mesh):
    in_specs = (
        P("node", None, None),
        P("node", None),
        P("node", None),
        P("node", None),
        P("node", None),
        P(),
    )
    return jax.shard_map(
        on_device, mesh=mesh, in_specs=in_specs, out_specs=P("node", "sector", None), check_vma=False
    )
```

```python
import functools
import types

import jax
import jax.numpy as jnp
from jax import lax
from jax.experimental import pallas as pl
from jax.experimental.pallas import tpu as pltpu
from jax.sharding import PartitionSpec as P

F32 = jnp.float32
BF = jnp.bfloat16


def sub(x, k):
    return jnp.broadcast_to(x[k : k + 1, :], (8, 128))


def lane(x, k):
    return jnp.broadcast_to(x[:, k : k + 1], (8, 128))


def eliminate(p, pi, near, g, row):
    c = [lane(p, 8 * g + m) for m in range(8)]
    cs = [[lane(a, 8 * g + m) for m in range(8)] for a, _ in near]
    near = [list(x) for x in near]
    pivots = jnp.ones((8, 128), F32)
    for k in range(0, 8, 2):
        a, b, d = sub(c[k], k), sub(c[k + 1], k), sub(c[k + 1], k + 1)
        det = a * d - b * b
        ia = 1.0 / a
        id1 = a * (1.0 / det)
        ratio = b * ia
        m0 = jnp.where(row > k, c[k] * ia, 0.0)
        m1 = jnp.where(row > k + 1, (c[k + 1] - c[k] * ratio) * id1, 0.0)
        p0, pi0 = sub(p, k), sub(pi, k)
        p1, pi1 = sub(p, k + 1) - ratio * p0, sub(pi, k + 1) - ratio * pi0
        es = {}
        for m in range(k + 2, 8):
            e0 = sub(c[m], k)
            es[m] = (e0, sub(c[m], k + 1) - ratio * e0)
            c[m] = c[m] - m0 * es[m][0] - m1 * es[m][1]
        p = p - m0 * p0 - m1 * p1
        pi = pi - m0 * pi0 - m1 * pi1
        for x, cr in zip(near, cs):
            n0 = cr[k] * ia
            n1 = (cr[k + 1] - cr[k] * ratio) * id1
            for m in range(k + 2, 8):
                cr[m] = cr[m] - n0 * es[m][0] - n1 * es[m][1]
            x[0] = x[0] - n0 * p0 - n1 * p1
            x[1] = x[1] - n0 * pi0 - n1 * pi1
        pivots = jnp.where(row == k, a, jnp.where(row == k + 1, det * ia, pivots))
    scale = lax.rsqrt(pivots)
    return p * scale, pi * scale, near


def chol128(load, u_ref, inv_ref):
    row = lax.broadcasted_iota(jnp.int32, (8, 128), 0)
    col = lax.broadcasted_iota(jnp.int32, (8, 128), 1)
    n = 4
    wa = [load(g) for g in range(16)]
    wi = [jnp.where(col == row + 8 * g, 1.0, 0.0).astype(F32) for g in range(16)]
    for start in range(0, 16, n):
        qs, qis = [], []
        for g in range(start, start + n):
            near = [(wa[x], wi[x]) for x in range(g + 1, start + n)]
            q, qi, near = eliminate(wa[g], wi[g], near, g, row)
            for x, (a, b) in zip(range(g + 1, start + n), near):
                wa[x], wi[x] = a, b
            q = jnp.where(col >= row + 8 * g, q, 0.0)
            u_ref[8 * g : 8 * g + 8, :] = q
            inv_ref[8 * g : 8 * g + 8, :] = qi
            qs.append(q)
            qis.append(qi)
        if start + n < 16:
            q = jnp.concatenate(qs, axis=0)
            full = jnp.concatenate([q, jnp.concatenate(qis, axis=0)], axis=1)
            qh = full.astype(BF)
            ql = (full - qh.astype(F32)).astype(BF)
            left = jnp.concatenate([qh[:, :128], ql[:, :128], qh[:, :128]], axis=0)
            right = jnp.concatenate([qh, qh, ql], axis=0)
            moved = lax.dot_general(left, right, (((0,), (0,)), ((), ())), preferred_element_type=F32)
            for x in range(start + n, 16):
                wa[x] = wa[x] - moved[8 * x : 8 * x + 8, :128]
                wi[x] = wi[x] - moved[8 * x : 8 * x + 8, 128:]


NT = (((1,), (1,)), ((), ()))
NN = (((1,), (0,)), ((), ()))


def dot(a, b, dims):
    return lax.dot_general(a, b, dims, preferred_element_type=F32)


def split(x):
    high = x.astype(BF)
    return high, (x - high.astype(F32)).astype(BF)


def dot3(a, b, dims):
    ah, al = split(a)
    bh, bl = split(b)
    return dot(ah, bh, dims) + (dot(al, bh, dims) + dot(ah, bl, dims))


def tile(i, size=256):
    return pl.ds(pl.multiple_of(i * size, size), size)


def span(start, size, m=128):
    return pl.ds(pl.multiple_of(start, m), size)


def column(row_ref, cols):
    return jnp.broadcast_to(row_ref[:, cols], (256, 256)).T


def make_normal(c, lo, hi):
    ir = lax.broadcasted_iota(jnp.int32, (256, 256), 0)
    ic = lax.broadcasted_iota(jnp.int32, (256, 256), 1)
    eye = jnp.where(ir == ic, 1.0, 0.0).astype(BF)
    depth = c.r.shape[1]

    def strip(i, _):
        for part in range(depth // 512):
            rows = slice(part * 512, (part + 1) * 512)
            c.rt[:, rows] = dot(eye, c.r[i, rows, :], NT).astype(BF)
        ri = tile(i)
        labels = column(c.lrow, ri)
        loading = column(c.frow, ri)

        def block(k, _):
            ki = tile(k)
            total = dot(c.rt[...], c.r[k], NN)
            total = total + jnp.where(labels == c.lrow[:, ki], loading * c.frow[:, ki], 0.0)
            total = total + jnp.where((ir == ic) & (i == k), c.vrow[:, ki], 0.0)
            c.a[ri, ki] = total
            return 0

        lax.fori_loop(0, i + 1, block, 0)
        return 0

    lax.fori_loop(lo, hi, strip, 0)


def diagonal_first(c, p):
    c0 = span(p * 256, 128)
    chol128(lambda g: c.a[span(p * 256 + 8 * g, 8, 8), c0], c.u0, c.i0)


def diagonal_second(c, p):
    c0, c1 = span(p * 256, 128), span(p * 256 + 128, 128)
    below = dot3(c.a[c1, c0], c.i0[...], NT)
    c.a[c1, c1] = c.a[c1, c1] - dot3(below, below, NT)
    chol128(lambda g: c.a[span(p * 256 + 128 + 8 * g, 8, 8), c1], c.u1, c.i1)
    c.a[c1, c0] = below
    c.a[c0, c0] = c.u0[...].T
    c.a[c1, c1] = c.u1[...].T
    corner = -dot3(c.i1[...], dot3(below, c.i0[...], NN), NN)
    zero = jnp.zeros((128, 128), F32)
    for rs, cs, v in ((0, 0, c.i0[...]), (0, 128, zero), (128, 0, corner), (128, 128, c.i1[...])):
        high, low = split(v)
        for at, part in ((0, high), (256, high), (512, low)):
            c.inv[p, rs : rs + 128, at + cs : at + cs + 128] = part


def finish_row(c, t):
    ti = tile(t)

    def panel(q, _):
        qi = tile(q)
        high, low = split(c.a[ti, qi])
        x = dot(jnp.concatenate([high, low, high], axis=1), c.inv[q], NT)
        c.a[ti, qi] = x
        high, low = split(x)
        c.lh[ti, qi] = high
        c.ll[ti, qi] = low

        def take_off(k, wide):
            ki = span(k * 256, wide)
            left, left_low = c.lh[ti, qi], c.ll[ti, qi]
            other, other_low = c.lh[ki, qi], c.ll[ki, qi]
            c.a[ti, ki] = c.a[ti, ki] - dot(
                jnp.concatenate([left, left_low, left], axis=1),
                jnp.concatenate([other, other, other_low], axis=1), NT)

        count = t - q

        @pl.when(count % 2 == 1)
        def _():
            take_off(q + 1, 256)

        def pair(e, _):
            take_off(q + 1 + count % 2 + 2 * e, 512)
            return 0

        lax.fori_loop(0, count // 2, pair, 0)
        return 0

    lax.fori_loop(0, t, panel, 0)


def write_band(c, s):
    n = c.a.shape[1]

    def rows(b, _):
        r0 = s * 512 + b * 64
        rr = lax.broadcasted_iota(jnp.int32, (64, n), 0) + r0
        cc = lax.broadcasted_iota(jnp.int32, (64, n), 1)
        c.o[tile(b, 64), :] = jnp.where(cc <= rr, c.a[span(r0, 64, 64), :], 0.0)
        return 0

    lax.fori_loop(0, 8, rows, 0)


def factor_scratch(n, rows):
    square = pltpu.VMEM((128, 128), F32)
    return dict(
        a=pltpu.VMEM((n, n), F32), rt=pltpu.VMEM((256, rows), BF),
        lh=pltpu.VMEM((n, n), BF), ll=pltpu.VMEM((n, n), BF),
        u0=square, u1=square, i0=square, i1=square,
        inv=pltpu.VMEM((n // 256, 256, 768), BF),
    )


def factor_steps(c, needs, arrived, forward, pass_on):
    def row(t, _):
        def if_needed(step):
            @pl.when(needs(t))
            def _():
                step()

        arrived(t)
        forward(t + 2, 0)
        if_needed(lambda: make_normal(c, t, t + 1))
        pass_on(t + 1, 1)
        if_needed(lambda: finish_row(c, t))
        forward(t + 2, 1)
        if_needed(lambda: diagonal_first(c, t))
        pass_on(t + 2, 0)
        if_needed(lambda: diagonal_second(c, t))
        return 0

    lax.fori_loop(0, 8, row, 0)


MESH = pl.DeviceIdType.MESH


def prep_kernel(at_ref, targets_ref, scale_ref, x_ref, o_ref, picks, scale):
    strip = pl.program_id(0)
    rows, children, width = x_ref.shape

    @pl.when(strip == 0)
    def _():
        targets = targets_ref[...]
        across = jnp.broadcast_to(targets.astype(F32), (children, children))
        first = lax.broadcasted_iota(jnp.int32, (children, children), 0)
        second = lax.broadcasted_iota(jnp.int32, (children, children), 1)
        earlier = (across.T == across) & (first < second)
        position = jnp.sum(jnp.where(earlier, 1.0, 0.0), axis=0, keepdims=True).astype(jnp.int32)
        slot = targets * 4 + position
        scale[...] = jnp.concatenate([scale_ref[...], jnp.zeros((16 - rows, children), F32)], axis=0).T
        height = picks.shape[0]
        out_row = lax.broadcasted_iota(jnp.int32, (height, children), 0)
        row_slot = (out_row // 16) * 4 + out_row % 4
        hit = row_slot == jnp.broadcast_to(slot, (height, children))
        lane_of = (out_row // 4) % 4
        for k in range(4):
            picks[:, k * children : (k + 1) * children] = jnp.where(hit & (lane_of == k), 1.0, 0.0).astype(BF)

    for quad in range(rows // 4):
        scaled = []
        for k in range(4):
            r = quad * 4 + k
            scaled.append((scale[:, r : r + 1] * x_ref[r].astype(F32)).astype(BF))
        scaled = jnp.concatenate(scaled, axis=0)
        chosen = []
        for b in range(2):
            plane = lax.rem(at_ref[1] + 8 - (lax.rem(at_ref[0] + strip, 4) + 4 * b), 8)
            chosen.append(picks[span(plane * 128, 128), :])
        moved = dot(jnp.concatenate(chosen, axis=0), scaled, NN).astype(BF)
        o_ref[:, quad * 16 : (quad + 1) * 16, :] = moved.reshape(16, 16, width)


def prepare(at, targets, scale, planes):
    rows, children, assets = planes.shape
    width = 256
    return pl.pallas_call(
        prep_kernel,
        out_shape=jax.ShapeDtypeStruct((128, rows * 4, width), BF),
        grid_spec=pltpu.PrefetchScalarGridSpec(
            num_scalar_prefetch=1,
            grid=(assets // width,),
            in_specs=[
                pl.BlockSpec((1, children), lambda i, s: (0, 0)),
                pl.BlockSpec((rows, children), lambda i, s: (0, 0)),
                pl.BlockSpec((rows, children, width), lambda i, s: (0, 0, i)),
            ],
            out_specs=pl.BlockSpec((16, rows * 4, width), lambda i, s: (i, 0, 0)),
            scratch_shapes=[pltpu.VMEM((1024, 4 * children), BF), pltpu.VMEM((children, 16), F32)],
        ),
    )(at, targets, scale, planes)


NAMES = ("a", "rt", "lh", "ll", "u0", "u1", "i0", "i1", "inv")


def main_kernel(out_ref, lrow, frow, vrow, o_ref, r, ls, ss, rs, ys, yr, zs, zr, *scratch):
    n = lax.axis_index("node")
    s = lax.axis_index("sector")
    z, w = n // 8, n % 8
    there = ((s + 1) % 4, (s + 3) % 4)
    c = types.SimpleNamespace(
        r=r, lrow=lrow, frow=frow, vrow=vrow, o=o_ref, **dict(zip(NAMES, scratch)))

    def distance(t, b, sector):
        return (sector + t) % 4 + 4 * b

    def send(h, t, b, i):
        j = distance(t, b, s)
        other = (w + i) % 8
        pltpu.make_async_remote_copy(
            out_ref.at[(2 * t + b) * 8 + other], r.at[t, tile(n, 48)], ss.at[h], rs.at[t, b],
            device_id=(((z + 8 - j) % 8) * 8 + other, s), device_id_type=MESH).start()

    def landed(t, b, count):
        rows = r.at[t, span(((z + distance(t, b, s)) % 8) * 384, 48 * count, 48)]
        pltpu.make_async_remote_copy(
            rows, rows, ss.at[0], rs.at[t, b], device_id=(n, there[0]), device_id_type=MESH).wait_recv()

    def group(t, b, sector, d, sent, got):
        rows = r.at[t, tile((z + distance(t, b, sector)) % 8, 384)]
        return pltpu.make_async_remote_copy(
            rows, rows, sent, got, device_id=(n, there[d]), device_id_type=MESH)

    def own(t, b, d):
        return group(t, b, s, d, ys.at[t, d, b], yr.at[t, d, b])

    def arriving(t, b, d):
        return group(t, b, there[1 - d], d, ys.at[t, d, b], yr.at[t, d, b])

    def relay(t, b):
        return group(t, b, there[1 - b], b, zs.at[t, b], zr.at[t, b])

    def relayed(t, b):
        return group(t, b, (s + 2) % 4, b, zs.at[t, b], zr.at[t, b])

    def kept(h):
        t = (4 - s) % 4 + 4 * h
        return pltpu.make_async_copy(out_ref.at[16 * t + w], r.at[t, tile(n, 48)], ls.at[h])

    def needs(t, sector):
        return 2 * sector + 1 >= t

    def wanted(t, b, d):
        if b == d:
            return needs(t, there[d]) | needs(t, (s + 2) % 4)
        return needs(t, there[d])

    def forward(t, b):
        @pl.when(t < 8)
        def _():
            if b:
                landed(t, 1, 8)
            else:
                @pl.when(distance(t, 0, s) == 0)
                def _():
                    landed(t, 0, 7)
                    kept(t // 4).wait()

                @pl.when(distance(t, 0, s) > 0)
                def _():
                    landed(t, 0, 8)

            for d in range(2):
                @pl.when(wanted(t, b, d))
                def _(d=d):
                    own(t, b, d).start()

    def pass_on(t, b):
        @pl.when(t < 8)
        def _():
            @pl.when(needs(t, s) | needs(t, there[b]))
            def _():
                arriving(t, b, b).wait_recv()

            @pl.when(needs(t, there[b]))
            def _():
                relay(t, b).start()

    def arrived(t):
        @pl.when(needs(t, s))
        def _():
            for b in range(2):
                arriving(t, b, 1 - b).wait_recv()
                relayed(t, b).wait_recv()

    for h in range(2):
        kept(h).start()

        def strip(t, _, h=h):
            for b in range(2):
                def one(i, _, b=b):
                    send(h, t, b, i)
                    return 0

                lax.fori_loop((8 - distance(t, b, s)) // 8, 8, one, 0)
            return 0

        lax.fori_loop(4 * h, 4 * h + 4, strip, 0)

    first, second = jnp.int32(0), jnp.int32(1)
    forward(first, 0)
    forward(first, 1)
    pass_on(first, 0)
    forward(second, 0)
    pass_on(first, 1)
    forward(second, 1)
    pass_on(second, 0)
    factor_steps(c, lambda t: needs(t, s), arrived, forward, pass_on)
    write_band(c, s)

    for h in range(2):
        blocks = out_ref.at[pl.ds(0, 63)]
        pltpu.make_async_remote_copy(
            blocks, blocks, ss.at[h], rs.at[0, 0], device_id=(n, there[0]), device_id_type=MESH
        ).wait_send()
    def sent(t, _):
        for b in range(2):
            for d in range(2):
                @pl.when(wanted(t, b, d))
                def _(b=b, d=d):
                    own(t, b, d).wait_send()

            @pl.when(needs(t, there[b]))
            def _(b=b):
                relay(t, b).wait_send()
        return 0

    lax.fori_loop(0, 8, sent, 0)


def exchange_and_factor(outbox, labels, loading, variance):
    dma = pltpu.SemaphoreType.DMA
    n = labels.shape[0]
    rows = outbox.shape[1] * 64
    vmem = pl.BlockSpec(memory_space=pltpu.VMEM)
    scratch = factor_scratch(n, rows)
    return pl.pallas_call(
        main_kernel,
        out_shape=jax.ShapeDtypeStruct((n // 4, n), F32),
        in_specs=[pl.BlockSpec(memory_space=pl.ANY)] + [vmem] * 3,
        out_specs=vmem,
        scratch_shapes=[pltpu.VMEM((8, rows, 256), BF), dma((2,)), dma((2,)), dma((8, 2)), dma((8, 2, 2)),
                        dma((8, 2, 2)), dma((8, 2)), dma((8, 2))] + [scratch[k] for k in NAMES],
        compiler_params=pltpu.CompilerParams(has_side_effects=True, vmem_limit_bytes=63 * 1024 * 1024),
    )(outbox, labels.astype(F32)[None, :], loading[None, :], variance[None, :])


def sector_labels(sector_sizes, count):
    sector_ends = jnp.cumsum(sector_sizes)
    asset_index = jnp.arange(count, dtype=jnp.int32)
    return jnp.sum((asset_index[:, None] >= sector_ends[None, :]).astype(jnp.int32), axis=1)


def on_device(returns, barrier_scale, parent_ids, loadings, own_variance, sector_sizes):
    child_count, row_count, asset_count = returns.shape
    at = jnp.stack([lax.axis_index("sector"), lax.axis_index("node") // 8]).astype(jnp.int32)
    outbox = prepare(
        at,
        parent_ids.reshape(1, child_count),
        jnp.sqrt(barrier_scale).T,
        returns.transpose(1, 0, 2),
    )
    labels = sector_labels(sector_sizes, asset_count)
    out = exchange_and_factor(outbox, labels, loadings[0], own_variance[0])
    return out[None]


def solution(mesh):
    in_specs = (
        P("node", None, None),
        P("node", None),
        P("node", None),
        P("node", None),
        P("node", None),
        P(),
    )
    return jax.shard_map(
        on_device, mesh=mesh, in_specs=in_specs, out_specs=P("node", "sector", None), check_vma=False
    )
```

```python
import functools
import types

import jax
import jax.numpy as jnp
from jax import lax
from jax.experimental import pallas as pl
from jax.experimental.pallas import tpu as pltpu
from jax.sharding import PartitionSpec as P

F32 = jnp.float32
BF = jnp.bfloat16


def sub(x, k):
    return jnp.broadcast_to(x[k : k + 1, :], (8, 128))


def lane(x, k):
    return jnp.broadcast_to(x[:, k : k + 1], (8, 128))


def eliminate(p, pi, near, g, row):
    c = [lane(p, 8 * g + m) for m in range(8)]
    cs = [[lane(a, 8 * g + m) for m in range(8)] for a, _ in near]
    near = [list(x) for x in near]
    pivots = jnp.ones((8, 128), F32)
    for k in range(0, 8, 2):
        a, b, d = sub(c[k], k), sub(c[k + 1], k), sub(c[k + 1], k + 1)
        det = a * d - b * b
        ia = 1.0 / a
        id1 = a * (1.0 / det)
        ratio = b * ia
        m0 = jnp.where(row > k, c[k] * ia, 0.0)
        m1 = jnp.where(row > k + 1, (c[k + 1] - c[k] * ratio) * id1, 0.0)
        p0, pi0 = sub(p, k), sub(pi, k)
        p1, pi1 = sub(p, k + 1) - ratio * p0, sub(pi, k + 1) - ratio * pi0
        es = {}
        for m in range(k + 2, 8):
            e0 = sub(c[m], k)
            es[m] = (e0, sub(c[m], k + 1) - ratio * e0)
            c[m] = c[m] - m0 * es[m][0] - m1 * es[m][1]
        p = p - m0 * p0 - m1 * p1
        pi = pi - m0 * pi0 - m1 * pi1
        for x, cr in zip(near, cs):
            n0 = cr[k] * ia
            n1 = (cr[k + 1] - cr[k] * ratio) * id1
            for m in range(k + 2, 8):
                cr[m] = cr[m] - n0 * es[m][0] - n1 * es[m][1]
            x[0] = x[0] - n0 * p0 - n1 * p1
            x[1] = x[1] - n0 * pi0 - n1 * pi1
        pivots = jnp.where(row == k, a, jnp.where(row == k + 1, det * ia, pivots))
    scale = lax.rsqrt(pivots)
    return p * scale, pi * scale, near


def chol128(load, u_ref, inv_ref):
    row = lax.broadcasted_iota(jnp.int32, (8, 128), 0)
    col = lax.broadcasted_iota(jnp.int32, (8, 128), 1)
    n = 4
    wa = [load(g) for g in range(16)]
    wi = [jnp.where(col == row + 8 * g, 1.0, 0.0).astype(F32) for g in range(16)]
    for start in range(0, 16, n):
        qs, qis = [], []
        for g in range(start, start + n):
            near = [(wa[x], wi[x]) for x in range(g + 1, start + n)]
            q, qi, near = eliminate(wa[g], wi[g], near, g, row)
            for x, (a, b) in zip(range(g + 1, start + n), near):
                wa[x], wi[x] = a, b
            q = jnp.where(col >= row + 8 * g, q, 0.0)
            u_ref[8 * g : 8 * g + 8, :] = q
            inv_ref[8 * g : 8 * g + 8, :] = qi
            qs.append(q)
            qis.append(qi)
        if start + n < 16:
            q = jnp.concatenate(qs, axis=0)
            full = jnp.concatenate([q, jnp.concatenate(qis, axis=0)], axis=1)
            qh = full.astype(BF)
            ql = (full - qh.astype(F32)).astype(BF)
            left = jnp.concatenate([qh[:, :128], ql[:, :128], qh[:, :128]], axis=0)
            right = jnp.concatenate([qh, qh, ql], axis=0)
            moved = lax.dot_general(left, right, (((0,), (0,)), ((), ())), preferred_element_type=F32)
            for x in range(start + n, 16):
                wa[x] = wa[x] - moved[8 * x : 8 * x + 8, :128]
                wi[x] = wi[x] - moved[8 * x : 8 * x + 8, 128:]


NT = (((1,), (1,)), ((), ()))
NN = (((1,), (0,)), ((), ()))


def dot(a, b, dims):
    return lax.dot_general(a, b, dims, preferred_element_type=F32)


def split(x):
    high = x.astype(BF)
    return high, (x - high.astype(F32)).astype(BF)


def dot3(a, b, dims):
    ah, al = split(a)
    bh, bl = split(b)
    return dot(ah, bh, dims) + (dot(al, bh, dims) + dot(ah, bl, dims))


def tile(i, size=256):
    return pl.ds(pl.multiple_of(i * size, size), size)


def span(start, size, m=128):
    return pl.ds(pl.multiple_of(start, m), size)


def column(row_ref, cols):
    return jnp.broadcast_to(row_ref[:, cols], (256, 256)).T


def make_normal(c, lo, hi):
    ir = lax.broadcasted_iota(jnp.int32, (256, 256), 0)
    ic = lax.broadcasted_iota(jnp.int32, (256, 256), 1)
    eye = jnp.where(ir == ic, 1.0, 0.0).astype(BF)
    depth = c.r.shape[1]

    def strip(i, _):
        for part in range(depth // 512):
            rows = slice(part * 512, (part + 1) * 512)
            c.rt[:, rows] = dot(eye, c.r[i, rows, :], NT).astype(BF)
        ri = tile(i)
        labels = column(c.lrow, ri)
        loading = column(c.frow, ri)

        def block(k, _):
            ki = tile(k)
            total = dot(c.rt[...], c.r[k], NN)
            total = total + jnp.where(labels == c.lrow[:, ki], loading * c.frow[:, ki], 0.0)
            total = total + jnp.where((ir == ic) & (i == k), c.vrow[:, ki], 0.0)
            c.a[ri, ki] = total
            return 0

        lax.fori_loop(0, i + 1, block, 0)
        return 0

    lax.fori_loop(lo, hi, strip, 0)


def diagonal_first(c, p):
    c0 = span(p * 256, 128)
    chol128(lambda g: c.a[span(p * 256 + 8 * g, 8, 8), c0], c.u0, c.i0)


def diagonal_second(c, p):
    c0, c1 = span(p * 256, 128), span(p * 256 + 128, 128)
    below = dot3(c.a[c1, c0], c.i0[...], NT)
    c.a[c1, c1] = c.a[c1, c1] - dot3(below, below, NT)
    chol128(lambda g: c.a[span(p * 256 + 128 + 8 * g, 8, 8), c1], c.u1, c.i1)
    c.a[c1, c0] = below
    c.a[c0, c0] = c.u0[...].T
    c.a[c1, c1] = c.u1[...].T
    corner = -dot3(c.i1[...], dot3(below, c.i0[...], NN), NN)
    zero = jnp.zeros((128, 128), F32)
    for rs, cs, v in ((0, 0, c.i0[...]), (0, 128, zero), (128, 0, corner), (128, 128, c.i1[...])):
        high, low = split(v)
        for at, part in ((0, high), (256, high), (512, low)):
            c.inv[p, rs : rs + 128, at + cs : at + cs + 128] = part


def finish_row(c, t):
    ti = tile(t)

    def panel(q, _):
        qi = tile(q)
        high, low = split(c.a[ti, qi])
        x = dot(jnp.concatenate([high, low, high], axis=1), c.inv[q], NT)
        c.a[ti, qi] = x
        high, low = split(x)
        c.lh[ti, qi] = high
        c.ll[ti, qi] = low

        def take_off(k, wide):
            ki = span(k * 256, wide)
            left, left_low = c.lh[ti, qi], c.ll[ti, qi]
            other, other_low = c.lh[ki, qi], c.ll[ki, qi]
            c.a[ti, ki] = c.a[ti, ki] - dot(
                jnp.concatenate([left, left_low, left], axis=1),
                jnp.concatenate([other, other, other_low], axis=1), NT)

        count = t - q

        @pl.when(count % 2 == 1)
        def _():
            take_off(q + 1, 256)

        @pl.when((count // 2) % 2 == 1)
        def _():
            take_off(q + 1 + count % 2, 512)

        @pl.when(count > 3)
        def _():
            take_off(t - 3, 1024)

        return 0

    lax.fori_loop(0, t, panel, 0)


def write_band(c, s):
    n = c.a.shape[1]

    def rows(b, _):
        r0 = s * 512 + b * 64
        rr = lax.broadcasted_iota(jnp.int32, (64, n), 0) + r0
        cc = lax.broadcasted_iota(jnp.int32, (64, n), 1)
        c.o[tile(b, 64), :] = jnp.where(cc <= rr, c.a[span(r0, 64, 64), :], 0.0)
        return 0

    lax.fori_loop(0, 8, rows, 0)


def factor_scratch(n, rows):
    square = pltpu.VMEM((128, 128), F32)
    return dict(
        a=pltpu.VMEM((n, n), F32), rt=pltpu.VMEM((256, rows), BF),
        lh=pltpu.VMEM((n, n), BF), ll=pltpu.VMEM((n, n), BF),
        u0=square, u1=square, i0=square, i1=square,
        inv=pltpu.VMEM((n // 256, 256, 768), BF),
    )


def factor_steps(c, needs, arrived, forward, pass_on):
    def row(t, _):
        def if_needed(step):
            @pl.when(needs(t))
            def _():
                step()

        arrived(t)
        forward(t + 2, 0)
        if_needed(lambda: make_normal(c, t, t + 1))
        pass_on(t + 1, 1)
        if_needed(lambda: finish_row(c, t))
        forward(t + 2, 1)
        if_needed(lambda: diagonal_first(c, t))
        pass_on(t + 2, 0)
        if_needed(lambda: diagonal_second(c, t))
        return 0

    lax.fori_loop(0, 8, row, 0)


MESH = pl.DeviceIdType.MESH


def prep_kernel(at_ref, targets_ref, scale_ref, x_ref, o_ref, picks, scale):
    strip = pl.program_id(0)
    rows, children, width = x_ref.shape

    @pl.when(strip == 0)
    def _():
        targets = targets_ref[...]
        across = jnp.broadcast_to(targets.astype(F32), (children, children))
        first = lax.broadcasted_iota(jnp.int32, (children, children), 0)
        second = lax.broadcasted_iota(jnp.int32, (children, children), 1)
        earlier = (across.T == across) & (first < second)
        position = jnp.sum(jnp.where(earlier, 1.0, 0.0), axis=0, keepdims=True).astype(jnp.int32)
        slot = targets * 4 + position
        scale[...] = jnp.concatenate([scale_ref[...], jnp.zeros((16 - rows, children), F32)], axis=0).T
        height = picks.shape[0]
        out_row = lax.broadcasted_iota(jnp.int32, (height, children), 0)
        row_slot = (out_row // 16) * 4 + out_row % 4
        hit = row_slot == jnp.broadcast_to(slot, (height, children))
        lane_of = (out_row // 4) % 4
        for k in range(4):
            picks[:, k * children : (k + 1) * children] = jnp.where(hit & (lane_of == k), 1.0, 0.0).astype(BF)

    for quad in range(rows // 4):
        scaled = []
        for k in range(4):
            r = quad * 4 + k
            scaled.append((scale[:, r : r + 1] * x_ref[r].astype(F32)).astype(BF))
        scaled = jnp.concatenate(scaled, axis=0)
        for b in range(2):
            plane = lax.rem(at_ref[1] + 8 - (lax.rem(at_ref[0] + strip, 4) + 4 * b), 8)
            moved = dot(picks[span(plane * 128, 128), :], scaled, NN).astype(BF)
            o_ref[8 * b : 8 * b + 8, quad * 16 : (quad + 1) * 16, :] = moved.reshape(8, 16, width)


def prepare(at, targets, scale, planes):
    rows, children, assets = planes.shape
    width = 256
    return pl.pallas_call(
        prep_kernel,
        out_shape=jax.ShapeDtypeStruct((128, rows * 4, width), BF),
        grid_spec=pltpu.PrefetchScalarGridSpec(
            num_scalar_prefetch=1,
            grid=(assets // width,),
            in_specs=[
                pl.BlockSpec((1, children), lambda i, s: (0, 0)),
                pl.BlockSpec((rows, children), lambda i, s: (0, 0)),
                pl.BlockSpec((rows, children, width), lambda i, s: (0, 0, i)),
            ],
            out_specs=pl.BlockSpec((16, rows * 4, width), lambda i, s: (i, 0, 0)),
            scratch_shapes=[pltpu.VMEM((1024, 4 * children), BF), pltpu.VMEM((children, 16), F32)],
        ),
    )(at, targets, scale, planes)


NAMES = ("a", "rt", "lh", "ll", "u0", "u1", "i0", "i1", "inv")


def main_kernel(out_ref, lrow, frow, vrow, o_ref, r, ls, ss, rs, ys, yr, zs, zr, *scratch):
    n = lax.axis_index("node")
    s = lax.axis_index("sector")
    z, w = n // 8, n % 8
    there = ((s + 1) % 4, (s + 3) % 4)
    c = types.SimpleNamespace(
        r=r, lrow=lrow, frow=frow, vrow=vrow, o=o_ref, **dict(zip(NAMES, scratch)))

    def distance(t, b, sector):
        return (sector + t) % 4 + 4 * b

    def send(h, t, b, i):
        j = distance(t, b, s)
        other = (w + i) % 8
        pltpu.make_async_remote_copy(
            out_ref.at[(2 * t + b) * 8 + other], r.at[t, tile(n, 48)], ss.at[h], rs.at[t, b],
            device_id=(((z + 8 - j) % 8) * 8 + other, s), device_id_type=MESH).start()

    def landed(t, b, count):
        rows = r.at[t, span(((z + distance(t, b, s)) % 8) * 384, 48 * count, 48)]
        pltpu.make_async_remote_copy(
            rows, rows, ss.at[0], rs.at[t, b], device_id=(n, there[0]), device_id_type=MESH).wait_recv()

    def group(t, b, sector, d, sent, got):
        rows = r.at[t, tile((z + distance(t, b, sector)) % 8, 384)]
        return pltpu.make_async_remote_copy(
            rows, rows, sent, got, device_id=(n, there[d]), device_id_type=MESH)

    def own(t, b, d):
        return group(t, b, s, d, ys.at[t, d, b], yr.at[t, d, b])

    def arriving(t, b, d):
        return group(t, b, there[1 - d], d, ys.at[t, d, b], yr.at[t, d, b])

    def relay(t, b):
        return group(t, b, there[1 - b], b, zs.at[t, b], zr.at[t, b])

    def relayed(t, b):
        return group(t, b, (s + 2) % 4, b, zs.at[t, b], zr.at[t, b])

    def kept(h):
        t = (4 - s) % 4 + 4 * h
        return pltpu.make_async_copy(out_ref.at[16 * t + w], r.at[t, tile(n, 48)], ls.at[h])

    def needs(t, sector):
        return 2 * sector + 1 >= t

    def wanted(t, b, d):
        if b == d:
            return needs(t, there[d]) | needs(t, (s + 2) % 4)
        return needs(t, there[d])

    def forward(t, b):
        @pl.when(t < 8)
        def _():
            if b:
                landed(t, 1, 8)
            else:
                @pl.when(distance(t, 0, s) == 0)
                def _():
                    landed(t, 0, 7)
                    kept(t // 4).wait()

                @pl.when(distance(t, 0, s) > 0)
                def _():
                    landed(t, 0, 8)

            for d in range(2):
                @pl.when(wanted(t, b, d))
                def _(d=d):
                    own(t, b, d).start()

    def pass_on(t, b):
        @pl.when(t < 8)
        def _():
            @pl.when(needs(t, s) | needs(t, there[b]))
            def _():
                arriving(t, b, b).wait_recv()

            @pl.when(needs(t, there[b]))
            def _():
                relay(t, b).start()

    def arrived(t):
        @pl.when(needs(t, s))
        def _():
            for b in range(2):
                arriving(t, b, 1 - b).wait_recv()
                relayed(t, b).wait_recv()

    for h in range(2):
        kept(h).start()

        def strip(t, _, h=h):
            for b in range(2):
                def one(i, _, b=b):
                    send(h, t, b, i)
                    return 0

                lax.fori_loop((8 - distance(t, b, s)) // 8, 8, one, 0)
            return 0

        lax.fori_loop(4 * h, 4 * h + 4, strip, 0)

    first, second = jnp.int32(0), jnp.int32(1)
    forward(first, 0)
    forward(first, 1)
    pass_on(first, 0)
    forward(second, 0)
    pass_on(first, 1)
    forward(second, 1)
    pass_on(second, 0)
    factor_steps(c, lambda t: needs(t, s), arrived, forward, pass_on)
    write_band(c, s)

    for h in range(2):
        blocks = out_ref.at[pl.ds(0, 63)]
        pltpu.make_async_remote_copy(
            blocks, blocks, ss.at[h], rs.at[0, 0], device_id=(n, there[0]), device_id_type=MESH
        ).wait_send()
    def sent(t, _):
        for b in range(2):
            for d in range(2):
                @pl.when(wanted(t, b, d))
                def _(b=b, d=d):
                    own(t, b, d).wait_send()

            @pl.when(needs(t, there[b]))
            def _(b=b):
                relay(t, b).wait_send()
        return 0

    lax.fori_loop(0, 8, sent, 0)


def exchange_and_factor(outbox, labels, loading, variance):
    dma = pltpu.SemaphoreType.DMA
    n = labels.shape[0]
    rows = outbox.shape[1] * 64
    vmem = pl.BlockSpec(memory_space=pltpu.VMEM)
    scratch = factor_scratch(n, rows)
    return pl.pallas_call(
        main_kernel,
        out_shape=jax.ShapeDtypeStruct((n // 4, n), F32),
        in_specs=[pl.BlockSpec(memory_space=pl.ANY)] + [vmem] * 3,
        out_specs=vmem,
        scratch_shapes=[pltpu.VMEM((8, rows, 256), BF), dma((2,)), dma((2,)), dma((8, 2)), dma((8, 2, 2)),
                        dma((8, 2, 2)), dma((8, 2)), dma((8, 2))] + [scratch[k] for k in NAMES],
        compiler_params=pltpu.CompilerParams(has_side_effects=True, vmem_limit_bytes=63 * 1024 * 1024),
    )(outbox, labels.astype(F32)[None, :], loading[None, :], variance[None, :])


def sector_labels(sector_sizes, count):
    sector_ends = jnp.cumsum(sector_sizes)
    asset_index = jnp.arange(count, dtype=jnp.int32)
    return jnp.sum((asset_index[:, None] >= sector_ends[None, :]).astype(jnp.int32), axis=1)


def on_device(returns, barrier_scale, parent_ids, loadings, own_variance, sector_sizes):
    child_count, row_count, asset_count = returns.shape
    at = jnp.stack([lax.axis_index("sector"), lax.axis_index("node") // 8]).astype(jnp.int32)
    outbox = prepare(
        at,
        parent_ids.reshape(1, child_count),
        jnp.sqrt(barrier_scale).T,
        returns.transpose(1, 0, 2),
    )
    labels = sector_labels(sector_sizes, asset_count)
    out = exchange_and_factor(outbox, labels, loadings[0], own_variance[0])
    return out[None]


def solution(mesh):
    in_specs = (
        P("node", None, None),
        P("node", None),
        P("node", None),
        P("node", None),
        P("node", None),
        P(),
    )
    return jax.shard_map(
        on_device, mesh=mesh, in_specs=in_specs, out_specs=P("node", "sector", None), check_vma=False
    )
```
